256 devices in a mesh: grp: 4 (over x), cell: 64 (over z, y, core).
Axes of the slice: x: 4, y: 4, z: 8, core: 2. Of those that a mesh axis runs over, the one named last changes fastest.
Arguments:
- fields: bfloat16 [512, 32, 65536], P('grp', None, 'cell'), may hold values from -6 to 6
- scales: float32 [512, 32, 512], P('grp', None, 'cell'), may hold values from 0.25 to 4
- pod_basis: bfloat16 [65536, 64], P('cell'), may hold values from -0.0234375 to 0.0234375
- param_order: int32 [30], replicated, may hold values from 0 to 29, each once
Outputs:
- sobol_maps: float32 [30, 65536], P(None, 'cell')
- total_map: float32 [65536], P('cell')
The draws below stay inside these ranges and needn't reach their ends.
Inputs may be any that keep to these rules, and one draw needn't show every extreme that they name: `param_order`: each parameter appears exactly once.
All inputs are finite; a program needn't handle non-finite values.
Results may differ from the reference program's by a relative error of at most 0.0003.
The reference program's roundings to bfloat16 on the way (of `dequant`) count: a program that leaves them out, or rounds other values in their place, can miss the bound.
Values sent between devices are 32-bit elements; how exact they have to be, the bound alone decides.
No kernel may reach another device: no remote copies, remote signals or barrier semaphores. Data moves between devices by JAX's collectives and lax.ppermute only.
A program may use at most 128 MiB of HBM per device.

```python
import math
import jax
import jax.numpy as jnp
from jax import lax

MODES = 64
PARAMS = 30
BLOCK = 128
ROW_GRP = 128
CELL_DEV = 1024
SLOTS = 32
ROWS = 512
CELLS = 65536
N_GRP = 4
N_CELL = 64


def block_scale(own_key, shape, cuts, smallest, largest):
    def one(position, shards_of):
        draws = jax.random.uniform(jax.random.fold_in(jax.random.fold_in(own_key, 6), position), (shards_of,), jnp.float32, smallest / len(cuts), largest / len(cuts))
        return jnp.repeat(jnp.exp(draws), shape[position] // shards_of).reshape((-1,) + (1,) * (len(shape) - position - 1))

    factor_of = one(*cuts[0])
    for cut in cuts[1:]:
        factor_of = factor_of * one(*cut)
    return factor_of


def bell_draw(stream_key, dims, deviation, limit, split=(), kind=jnp.bfloat16):
    level = block_scale(stream_key, dims, split, -0.22, 0.18) if split else 1.0
    result = jax.random.normal(stream_key, dims, jnp.float32) * deviation * level
    return jnp.minimum(jnp.maximum(result, -limit), limit).astype(kind)


def setup_inputs(seed: int = 0) -> dict:
    splits = jax.random.split(jax.random.key(seed), 5)
    return {
        "fields": bell_draw(splits[0], (ROWS, SLOTS, CELLS), 1.0, 6.0, ((0, 4), (2, 64))),
        "scales": jnp.clip(jnp.exp(math.log(4.0) - 2.7725887 * jax.random.uniform(splits[1], (ROWS, SLOTS, CELLS // BLOCK), jnp.float32) ** block_scale(splits[1], (ROWS, SLOTS, CELLS // BLOCK), ((0, 4), (2, 64)), -0.2, 0.2)), 0.25, 4.0),
        "pod_basis": bell_draw(splits[2], (CELLS, MODES), CELLS ** -0.5, 0.0234375, ((0, 64),)),
        "param_order": jax.random.permutation(splits[3], PARAMS).astype(jnp.int32),
    }


def project(piece, scale_piece, basis_piece):
    rows, slots, cells = piece.shape
    blocks = scale_piece.shape[2]
    dequant = (piece.astype(jnp.float32).reshape(rows, slots, blocks, cells // blocks) * scale_piece[..., None]).astype(jnp.bfloat16)
    flat = dequant.reshape(rows * slots, cells)
    return jnp.dot(flat, basis_piece, preferred_element_type=jnp.float32).reshape(rows, slots, basis_piece.shape[1])


def moments(coefficients):
    first = coefficients[:, 0]
    second_set = coefficients[:, 1]
    swapped = coefficients[:, 2:] - first[:, None, :]
    cross = jnp.einsum('rk,rpl->pkl', second_set, swapped, precision=lax.Precision.HIGHEST)
    squares = jnp.dot(first.T, first, precision=lax.Precision.HIGHEST) + jnp.dot(second_set.T, second_set, precision=lax.Precision.HIGHEST)
    column_sums = jnp.sum(first, axis=0) + jnp.sum(second_set, axis=0)
    return cross, squares, column_sums


def finish(cross, squares, column_sums, row_total, param_order, pod_basis, cell_total):
    count = param_order.shape[0]
    slot_cov = cross / row_total
    selector = (param_order[:, None] == jnp.arange(count).astype(jnp.int32)[None, :]).astype(jnp.float32)
    param_cov = jnp.einsum('sp,skl->pkl', selector, slot_cov, precision=lax.Precision.HIGHEST)
    average = column_sums / (2.0 * row_total)
    covariance = squares / (2.0 * row_total) - average[:, None] * average[None, :]
    stacked = jnp.concatenate([param_cov, covariance[None]], axis=0)
    phi = pod_basis.astype(jnp.float32)

    def one_map(matrix):
        return cell_total * jnp.sum(jnp.dot(phi, matrix, precision=lax.Precision.HIGHEST) * phi, axis=1)

    all_maps = lax.map(one_map, stacked)
    return all_maps[:-1], all_maps[-1]


def reference(fields, scales, pod_basis, param_order):
    row_total = ROW_GRP * N_GRP

    def add_shard(shard_index, total):
        first_cell = (shard_index * CELL_DEV).astype(jnp.int32)
        first_block = (shard_index * (CELL_DEV // BLOCK)).astype(jnp.int32)
        piece = lax.dynamic_slice_in_dim(fields, first_cell, CELL_DEV, 2)
        scale_piece = lax.dynamic_slice_in_dim(scales, first_block, CELL_DEV // BLOCK, 2)
        basis_piece = lax.dynamic_slice_in_dim(pod_basis, first_cell, CELL_DEV, 0)
        return total + project(piece, scale_piece, basis_piece)

    coefficients = lax.fori_loop(0, N_CELL, add_shard, jnp.zeros((row_total, SLOTS, MODES), jnp.float32))
    cross, squares, column_sums = moments(coefficients)
    return finish(cross, squares, column_sums, float(row_total), param_order, pod_basis, float(CELLS))
```

```python
import jax
import jax.numpy as jnp
from jax import lax
from jax.experimental import pallas as pl
from jax.experimental.pallas import tpu as pltpu
from jax.sharding import Mesh, PartitionSpec as P

HIGHEST = lax.Precision.HIGHEST
F32 = jnp.float32
BF16 = jnp.bfloat16
VMEM = pl.BlockSpec(memory_space=pltpu.VMEM)
SMEM = pl.BlockSpec(memory_space=pltpu.SMEM)


def project_kernel(half_ref, first_ref, second_ref, scale_ref, basis_ref, out_ref, by_block, dequant, weights):
    step = pl.program_id(0)
    rows, slots, cells = first_ref.shape
    blocks = scale_ref.shape[0] // slots
    lanes = cells // blocks
    modes = basis_ref.shape[0]
    packed = out_ref.shape[0] // slots

    @pl.when(step == 0)
    def _():
        for block in range(blocks):
            by_block[block] = scale_ref[pl.ds(block, slots, stride=blocks), :]
        turned = basis_ref[...].astype(F32).T.astype(BF16)
        weights[...] = jnp.zeros_like(weights)
        weights[:cells, :modes] = turned
        weights[cells:, modes:] = turned

    start = half_ref[0] * (2 * packed) + step * rows
    turn = lax.rem(128 - start, 128)
    for block in range(blocks):
        rolled = pltpu.roll(by_block[block], turn, 1)
        for which, source in enumerate((first_ref, second_ref)):
            for row in range(rows):
                lane = which * packed + row
                scale = jnp.broadcast_to(rolled[:, lane : lane + 1], (slots, lanes))
                piece = source[row, :, block * lanes : (block + 1) * lanes]
                column = which * cells + block * lanes
                dequant[row * slots : (row + 1) * slots, column : column + lanes] = (
                    piece.astype(F32) * scale
                ).astype(BF16)
    modes_out = jnp.dot(dequant[...], weights[...], preferred_element_type=F32)
    slot = lax.broadcasted_iota(jnp.int32, (slots, 2 * modes), 0)
    for row in range(rows):
        tile = modes_out[row * slots : (row + 1) * slots]
        tile = tile - jnp.where(slot >= 2, jnp.broadcast_to(tile[:1], tile.shape), 0.0)
        out_ref[pl.ds(step * rows + row, slots, stride=packed), :] = tile


def project(half, fields, scales, basis):
    rows, slots, cells = fields.shape
    modes = basis.shape[0]
    packed = rows // 4
    step = 8
    steps = packed // step
    grid_spec = pltpu.PrefetchScalarGridSpec(
        num_scalar_prefetch=1,
        grid=(steps,),
        in_specs=[
            pl.BlockSpec((step, slots, cells), lambda i, h: (h[0] * 2 * steps + i, 0, 0)),
            pl.BlockSpec((step, slots, cells), lambda i, h: (h[0] * 2 * steps + steps + i, 0, 0)),
            pl.BlockSpec(scales.shape, lambda i, h: (0, 0)),
            pl.BlockSpec(basis.shape, lambda i, h: (0, 0)),
        ],
        out_specs=pl.BlockSpec((slots * packed, 2 * modes), lambda i, h: (0, 0)),
        scratch_shapes=[
            pltpu.VMEM((scales.shape[0] // slots, slots, rows), F32),
            pltpu.VMEM((step * slots, 2 * cells), BF16),
            pltpu.VMEM((2 * cells, 2 * modes), BF16),
        ],
    )
    return pl.pallas_call(
        project_kernel,
        grid_spec=grid_spec,
        out_shape=jax.ShapeDtypeStruct((slots * packed, 2 * modes), F32),
        cost_estimate=pl.CostEstimate(
            flops=rows * slots * cells * modes, bytes_accessed=rows * slots * cells, transcendentals=0
        ),
        name="project",
    )(half, fields, fields, scales, basis)


def moments_kernel(where_ref, parts_ref, second_ref, keep_ref, send_ref):
    slot, half = where_ref[0], where_ref[1]
    own = parts_ref[0]
    for source in range(1, parts_ref.shape[0]):
        own = own + parts_ref[source]
    second = second_ref[0]
    for source in range(1, second_ref.shape[0]):
        second = second + second_ref[source]
    left = jnp.where(slot == 0, own, second)
    wide = lax.dot_general(left, own, (((0,), (0,)), ((), ())), precision=HIGHEST, preferred_element_type=F32)
    matrix = wide[:64, :64] + wide[64:, 64:]
    sums = jnp.sum(own, axis=0, keepdims=True)
    sums = sums[:, :64] + sums[:, 64:]
    low = jnp.concatenate([sums[:, 32:], sums[:, :32]], axis=1)
    row = lax.broadcasted_iota(jnp.int32, matrix.shape, 0)
    lane = lax.broadcasted_iota(jnp.int32, matrix.shape, 1)
    spare = (slot < 2) & (lane < 32)
    matrix = jnp.where(spare & (row == 32), jnp.broadcast_to(sums, matrix.shape), matrix)
    matrix = jnp.where(spare & (row == 33), jnp.broadcast_to(low, matrix.shape), matrix)
    upper = jnp.concatenate([matrix[:16], matrix[16:32]], axis=1)
    lower = jnp.concatenate([matrix[32:48], matrix[48:]], axis=1)
    keep_ref[...] = jnp.where(half == 0, upper, lower)
    send_ref[...] = jnp.where(half == 0, lower, upper)


def moments(where, parts, second):
    out = jax.ShapeDtypeStruct((16, 128), F32)
    return pl.pallas_call(
        moments_kernel,
        in_specs=[SMEM, VMEM, VMEM],
        out_specs=(VMEM, VMEM),
        out_shape=(out, out),
        name="moments",
    )(where, parts, second)


def three(value):
    high = value.astype(BF16)
    rest = value - high.astype(F32)
    middle = rest.astype(BF16)
    return high, middle, (rest - middle.astype(F32)).astype(BF16)


def maps_kernel(rows_total, cell_total, half_ref, order_ref, mine_ref, other_ref, basis_ref, maps_ref, total_ref):
    half = half_ref[0]
    mine, other = mine_ref[...], other_ref[...]
    halves = (jnp.where(half == 0, mine, other), jnp.where(half == 0, other, mine))
    slots = mine.shape[0]
    modes, cells = basis_ref.shape
    phi = basis_ref[...]
    none = jnp.zeros_like(phi)
    right_first = jnp.concatenate([phi, phi, phi, none], axis=0)
    right_second = jnp.concatenate([phi, phi, none, phi], axis=0)
    phi32 = phi.astype(F32)

    def quadratic(pieces):
        count = pieces[0].shape[0]
        result = None
        for part, piece in enumerate(pieces):
            flat = piece.reshape(count * 16, 128)
            lane = lax.broadcasted_iota(jnp.int32, flat.shape, 1)
            high = flat.astype(BF16).astype(F32)
            rest = flat - high
            middle = rest.astype(BF16).astype(F32)
            low = (rest - middle).astype(BF16)
            turned = pltpu.roll(middle, 64, 1)
            for side, right in enumerate((right_first, right_second)):
                front = jnp.where((lane < 64) == (side == 0), high, turned).astype(BF16)
                left = jnp.concatenate([front, low], axis=1)
                product = jnp.dot(left, right, preferred_element_type=F32).reshape(count, 16, cells)
                first = 32 * part + 16 * side
                term = jnp.sum(product * phi32[None, first : first + 16], axis=1)
                result = term if result is None else result + term
        return result

    group = 8
    for start in range(0, slots, group):
        found = cell_total / rows_total * quadratic([h[start : start + group] for h in halves])
        for slot in range(max(start, 2), start + group):
            maps_ref[pl.ds(order_ref[slot - 2], 1), :] = found[slot - start : slot - start + 1]

    both = [h[0] + h[1] for h in halves]
    sums = both[1][0:1, :64]
    low = both[1][1:2, :64]
    lane1 = lax.broadcasted_iota(jnp.int32, sums.shape, 1)
    sums = jnp.where(lane1 < 32, sums, jnp.concatenate([low[:, 32:], low[:, :32]], axis=1))
    average = sums / (2.0 * rows_total)
    outer = lax.dot_general(average, average, (((0,), (0,)), ((), ())), precision=HIGHEST, preferred_element_type=F32)
    lane = lax.broadcasted_iota(jnp.int32, both[0].shape, 1)
    column = jnp.where(lane < 64, lane, lane - 64)
    weight = jnp.where(column < 32, 1.0, 2.0)
    outer_upper = jnp.concatenate([outer[:16], outer[16:32]], axis=1)
    outer_lower = jnp.concatenate([outer[32:48], outer[48:]], axis=1)
    upper = (both[0] / (2.0 * rows_total) - outer_upper) * weight
    lower = jnp.where(column < 32, 0.0, both[1] / (2.0 * rows_total) - outer_lower)
    total = quadratic([upper[None], lower[None]])
    total_ref[...] = cell_total * total


def make_maps(rows_total, cell_total, half, order, mine, other, basis):
    cells = basis.shape[1]
    params = order.shape[0]

    def kernel(*refs):
        maps_kernel(rows_total, cell_total, *refs)

    return pl.pallas_call(
        kernel,
        in_specs=[SMEM, SMEM, VMEM, VMEM, VMEM],
        out_specs=(VMEM, VMEM),
        out_shape=(jax.ShapeDtypeStruct((params, cells), F32), jax.ShapeDtypeStruct((1, cells), F32)),
        name="maps",
    )(half, order, mine, other, basis)


def shifted(value, axis, size, shift):
    return lax.ppermute(value, axis, [(i, (i + shift) % size) for i in range(size)])


def on_device(fields, scales, pod_basis, param_order):
    rows, slots, cells = fields.shape
    blocks = scales.shape[2]
    modes = pod_basis.shape[1]
    sizes = {name: lax.axis_size(name) for name in ("grp", "z", "y", "core")}
    rows_total = float(rows * sizes["grp"])
    cell_total = float(cells * sizes["z"] * sizes["y"] * sizes["core"])
    core = lax.axis_index("core").astype(jnp.int32)
    slot = (lax.axis_index("z") * sizes["y"] + lax.axis_index("y")).astype(jnp.int32)
    by_slot = jnp.transpose(scales, (1, 2, 0)).reshape(slots * blocks, rows)
    basis = pod_basis.T
    packed = rows // 4

    theirs = project((1 - core)[None], fields, by_slot, basis)
    got = shifted(theirs, "core", 2, 1)
    ours = project(core[None], fields, by_slot, basis)
    halves = (ours + got).reshape(slots, packed, 2 * modes)

    parts = lax.all_to_all(halves, ("z", "y"), 0, 0, tiled=True)
    second = halves[1]
    second = second + sum(shifted(second, "y", sizes["y"], s) for s in range(1, sizes["y"]))
    second = jnp.broadcast_to(second[None], (sizes["z"], packed, 2 * modes))
    second = lax.all_to_all(second, "z", 0, 0, tiled=True)

    keep, send = moments(jnp.stack([slot, core]), parts, second)
    piece = keep + shifted(send, "core", 2, 1)
    piece = piece + sum(shifted(piece, "grp", sizes["grp"], s) for s in range(1, sizes["grp"]))
    copies = jnp.broadcast_to(piece[None], (slots,) + piece.shape)
    mine = lax.all_to_all(copies, ("z", "y"), 0, 0, tiled=True)
    other = shifted(mine, "core", 2, 1)
    sobol, total = make_maps(rows_total, cell_total, core[None], param_order, mine, other, basis)
    return sobol, total.reshape(cells)


def solution(mesh):
    split = Mesh(mesh.devices.reshape(4, 8, 4, 2), ("grp", "z", "y", "core"))
    cell = ("z", "y", "core")
    return jax.shard_map(
        on_device,
        mesh=split,
        in_specs=(P("grp", None, cell), P("grp", None, cell), P(cell, None), P()),
        out_specs=(P(None, cell), P(cell)),
        check_vma=False,
    )
```

```python
import functools

import jax
import jax.numpy as jnp
from jax import lax
from jax.experimental import pallas as pl
from jax.experimental.pallas import tpu as pltpu
from jax.sharding import Mesh, PartitionSpec as P

HIGHEST = lax.Precision.HIGHEST
F32 = jnp.float32
BF16 = jnp.bfloat16
VMEM = pl.BlockSpec(memory_space=pltpu.VMEM)
SMEM = pl.BlockSpec(memory_space=pltpu.SMEM)


def project_kernel(chunk, half_ref, fields_ref, scale_ref, basis_ref, out_ref, buffer, weights, spread, scales3, result, in_sems, out_sems):
    rows, slots, cells = buffer.shape
    packed = rows // 2
    modes = basis_ref.shape[0]
    blocks = scale_ref.shape[0] // slots
    lanes = cells // blocks
    chunks = packed // chunk
    base = half_ref[0] * rows

    def fetch(index, which):
        first = which * packed + index * chunk
        return pltpu.make_async_copy(
            fields_ref.at[pl.ds(base + first, chunk)], buffer.at[pl.ds(first, chunk)], in_sems.at[index, which]
        )

    def put(index):
        return pltpu.make_async_copy(
            result.at[index], out_ref.at[:, pl.ds(index * chunk, chunk)], out_sems.at[index]
        )

    for index in range(chunks):
        for which in range(2):
            fetch(index, which).start()

    turned = basis_ref[...].astype(F32).T.astype(BF16)
    none = jnp.zeros_like(turned)
    weights[0] = jnp.concatenate([turned, none], axis=1)
    weights[1] = jnp.concatenate([none, turned], axis=1)
    block_of_row = lax.broadcasted_iota(jnp.int32, (256, lanes), 0) % blocks
    for block in range(blocks):
        spread[:, block * lanes : (block + 1) * lanes] = jnp.where(block_of_row == block, 1.0, 0.0).astype(BF16)
    by_row = scale_ref[...].T
    high = by_row.astype(BF16).astype(F32)
    rest = by_row - high
    middle = rest.astype(BF16).astype(F32)
    low = rest - middle
    lane = lax.broadcasted_iota(jnp.int32, (by_row.shape[0], 128), 1)
    for column in range(2):
        cut = slice(column * 128, (column + 1) * 128)
        turned_middle = pltpu.roll(middle[:, cut], 64, 1)
        scales3[2 * column, :, :128] = jnp.where(lane < 64, high[:, cut], turned_middle)
        scales3[2 * column, :, 128:] = low[:, cut]
        scales3[2 * column + 1, :, :128] = jnp.where(lane < 64, turned_middle, high[:, cut])
        scales3[2 * column + 1, :, 128:] = low[:, cut]

    slot8 = lax.broadcasted_iota(jnp.int32, (8, 256), 0)
    lane8 = lax.broadcasted_iota(jnp.int32, (8, 256), 1)
    own = (lane8 % 64) // 8 == slot8
    masks = (own & (lane8 < 192), own & ((lane8 < 128) | (lane8 >= 192)))
    slot = lax.broadcasted_iota(jnp.int32, (slots, 2 * modes), 0)
    for index in range(chunks):
        total = None
        for which in range(2):
            fetch(index, which).wait()
            first = which * packed + index * chunk
            left = []
            for row in range(chunk):
                for q in range(slots // 8):
                    line = jnp.broadcast_to(scales3[q, pl.ds(base + first + row, 1), :], (8, 256))
                    left.append(jnp.where(masks[q % 2], line, 0.0))
            left = jnp.concatenate(left, axis=0).astype(BF16)
            scale = jnp.dot(left, spread[...], preferred_element_type=F32)
            piece = buffer[first : first + chunk].reshape(chunk * slots, cells)
            dequant = (piece.astype(F32) * scale).astype(BF16)
            part = jnp.dot(dequant, weights[which], preferred_element_type=F32)
            total = part if total is None else total + part
        for row in range(chunk):
            tile = total[row * slots : (row + 1) * slots]
            tile = tile - jnp.where(slot >= 2, jnp.broadcast_to(tile[:1], tile.shape), 0.0)
            result[index, :, row, :] = tile
        put(index).start()
    for index in range(chunks):
        put(index).wait()


def project(half, fields, scales, basis):
    rows, slots, cells = fields.shape
    modes = basis.shape[0]
    packed = rows // 4
    chunk = 8
    chunks = packed // chunk
    return pl.pallas_call(
        functools.partial(project_kernel, chunk),
        in_specs=[SMEM, pl.BlockSpec(memory_space=pltpu.HBM), VMEM, VMEM],
        out_specs=pl.BlockSpec(memory_space=pl.ANY),
        out_shape=jax.ShapeDtypeStruct((slots, packed, 2 * modes), F32),
        scratch_shapes=[
            pltpu.VMEM((rows // 2, slots, cells), BF16),
            pltpu.VMEM((2, cells, 2 * modes), BF16),
            pltpu.VMEM((256, cells), BF16),
            pltpu.VMEM((slots // 8, rows, 256), F32),
            pltpu.VMEM((chunks, slots, chunk, 2 * modes), F32),
            pltpu.SemaphoreType.DMA((chunks, 2)),
            pltpu.SemaphoreType.DMA((chunks,)),
        ],
        compiler_params=pltpu.CompilerParams(vmem_limit_bytes=32 << 20),
        cost_estimate=pl.CostEstimate(
            flops=rows * slots * cells * modes, bytes_accessed=rows * slots * cells, transcendentals=0
        ),
        name="project",
    )(half, fields, scales, basis)


def moments_kernel(where_ref, parts_ref, second_ref, keep_ref, send_ref):
    slot, half = where_ref[0], where_ref[1]
    own = parts_ref[0]
    for source in range(1, parts_ref.shape[0]):
        own = own + parts_ref[source]
    second = second_ref[0]
    for source in range(1, second_ref.shape[0]):
        second = second + second_ref[source]
    left = jnp.where(slot == 0, own, second)
    wide = lax.dot_general(left, own, (((0,), (0,)), ((), ())), precision=HIGHEST, preferred_element_type=F32)
    matrix = wide[:64, :64] + wide[64:, 64:]
    sums = jnp.sum(own, axis=0, keepdims=True)
    sums = sums[:, :64] + sums[:, 64:]
    low = jnp.concatenate([sums[:, 32:], sums[:, :32]], axis=1)
    row = lax.broadcasted_iota(jnp.int32, matrix.shape, 0)
    lane = lax.broadcasted_iota(jnp.int32, matrix.shape, 1)
    spare = (slot < 2) & (lane < 32)
    matrix = jnp.where(spare & (row == 32), jnp.broadcast_to(sums, matrix.shape), matrix)
    matrix = jnp.where(spare & (row == 33), jnp.broadcast_to(low, matrix.shape), matrix)
    upper = jnp.concatenate([matrix[:16], matrix[16:32]], axis=1)
    lower = jnp.concatenate([matrix[32:48], matrix[48:]], axis=1)
    keep_ref[...] = jnp.where(half == 0, upper, lower)
    send_ref[...] = jnp.where(half == 0, lower, upper)


def moments(where, parts, second):
    out = jax.ShapeDtypeStruct((16, 128), F32)
    return pl.pallas_call(
        moments_kernel,
        in_specs=[SMEM, VMEM, VMEM],
        out_specs=(VMEM, VMEM),
        out_shape=(out, out),
        compiler_params=pltpu.CompilerParams(vmem_limit_bytes=16 << 20),
        cost_estimate=pl.CostEstimate(flops=1 << 22, bytes_accessed=1 << 20, transcendentals=0),
        name="moments",
    )(where, parts, second)


def three(value):
    high = value.astype(BF16)
    rest = value - high.astype(F32)
    middle = rest.astype(BF16)
    return high, middle, (rest - middle.astype(F32)).astype(BF16)


def maps_kernel(rows_total, cell_total, half_ref, order_ref, mine_ref, other_ref, basis_ref, maps_ref, total_ref):
    half = half_ref[0]
    mine, other = mine_ref[...], other_ref[...]
    halves = (jnp.where(half == 0, mine, other), jnp.where(half == 0, other, mine))
    slots = mine.shape[0]
    modes, cells = basis_ref.shape
    phi = basis_ref[...]
    none = jnp.zeros_like(phi)
    right_first = jnp.concatenate([phi, phi, phi, none], axis=0)
    right_second = jnp.concatenate([phi, phi, none, phi], axis=0)
    phi32 = phi.astype(F32)

    def quadratic(pieces):
        count = pieces[0].shape[0]
        result = None
        for part, piece in enumerate(pieces):
            flat = piece.reshape(count * 16, 128)
            lane = lax.broadcasted_iota(jnp.int32, flat.shape, 1)
            high = flat.astype(BF16).astype(F32)
            rest = flat - high
            middle = rest.astype(BF16).astype(F32)
            low = (rest - middle).astype(BF16)
            turned = pltpu.roll(middle, 64, 1)
            for side, right in enumerate((right_first, right_second)):
                front = jnp.where((lane < 64) == (side == 0), high, turned).astype(BF16)
                left = jnp.concatenate([front, low], axis=1)
                product = jnp.dot(left, right, preferred_element_type=F32).reshape(count, 16, cells)
                first = 32 * part + 16 * side
                term = jnp.sum(product * phi32[None, first : first + 16], axis=1)
                result = term if result is None else result + term
        return result

    group = 8
    for start in range(0, slots, group):
        found = cell_total / rows_total * quadratic([h[start : start + group] for h in halves])
        for slot in range(max(start, 2), start + group):
            maps_ref[pl.ds(order_ref[slot - 2], 1), :] = found[slot - start : slot - start + 1]

    both = [h[0] + h[1] for h in halves]
    sums = both[1][0:1, :64]
    low = both[1][1:2, :64]
    lane1 = lax.broadcasted_iota(jnp.int32, sums.shape, 1)
    sums = jnp.where(lane1 < 32, sums, jnp.concatenate([low[:, 32:], low[:, :32]], axis=1))
    average = sums / (2.0 * rows_total)
    outer = lax.dot_general(average, average, (((0,), (0,)), ((), ())), precision=HIGHEST, preferred_element_type=F32)
    lane = lax.broadcasted_iota(jnp.int32, both[0].shape, 1)
    column = jnp.where(lane < 64, lane, lane - 64)
    weight = jnp.where(column < 32, 1.0, 2.0)
    outer_upper = jnp.concatenate([outer[:16], outer[16:32]], axis=1)
    outer_lower = jnp.concatenate([outer[32:48], outer[48:]], axis=1)
    upper = (both[0] / (2.0 * rows_total) - outer_upper) * weight
    lower = jnp.where(column < 32, 0.0, both[1] / (2.0 * rows_total) - outer_lower)
    total = quadratic([upper[None], lower[None]])
    total_ref[...] = cell_total * total


def make_maps(rows_total, cell_total, half, order, mine, other, basis):
    cells = basis.shape[1]
    params = order.shape[0]

    def kernel(*refs):
        maps_kernel(rows_total, cell_total, *refs)

    return pl.pallas_call(
        kernel,
        in_specs=[SMEM, SMEM, VMEM, VMEM, VMEM],
        out_specs=(VMEM, VMEM),
        out_shape=(jax.ShapeDtypeStruct((params, cells), F32), jax.ShapeDtypeStruct((1, cells), F32)),
        compiler_params=pltpu.CompilerParams(vmem_limit_bytes=32 << 20),
        cost_estimate=pl.CostEstimate(flops=1 << 28, bytes_accessed=1 << 20, transcendentals=0),
        name="maps",
    )(half, order, mine, other, basis)


def shifted(value, axis, size, shift):
    return lax.ppermute(value, axis, [(i, (i + shift) % size) for i in range(size)])


def on_device(fields, scales, pod_basis, param_order):
    rows, slots, cells = fields.shape
    blocks = scales.shape[2]
    modes = pod_basis.shape[1]
    sizes = {name: lax.axis_size(name) for name in ("grp", "z", "y", "core")}
    rows_total = float(rows * sizes["grp"])
    cell_total = float(cells * sizes["z"] * sizes["y"] * sizes["core"])
    core = lax.axis_index("core").astype(jnp.int32)
    slot = (lax.axis_index("z") * sizes["y"] + lax.axis_index("y")).astype(jnp.int32)
    by_slot = jnp.transpose(scales, (1, 2, 0)).reshape(slots * blocks, rows)
    basis = pod_basis.T
    packed = rows // 4

    theirs = project((1 - core)[None], fields, by_slot, basis)
    got = shifted(theirs, "core", 2, 1)
    ours = project(core[None], fields, by_slot, basis)
    halves = ours + got

    parts = lax.all_to_all(halves, ("z", "y"), 0, 0, tiled=True)
    second = halves[1]
    second = second + sum(shifted(second, "y", sizes["y"], s) for s in range(1, sizes["y"]))
    second = second + sum(shifted(second, "z", sizes["z"], s) for s in range(1, sizes["z"] // 2))
    second = jnp.stack([second, shifted(second, "z", sizes["z"], sizes["z"] // 2)])

    keep, send = moments(jnp.stack([slot, core]), parts, second)
    piece = keep + shifted(send, "core", 2, 1)
    piece = piece + sum(shifted(piece, "grp", sizes["grp"], s) for s in range(1, sizes["grp"]))
    copies = jnp.broadcast_to(piece[None], (slots,) + piece.shape)
    mine = lax.all_to_all(copies, ("z", "y"), 0, 0, tiled=True)
    other = shifted(mine, "core", 2, 1)
    sobol, total = make_maps(rows_total, cell_total, core[None], param_order, mine, other, basis)
    return sobol, total.reshape(cells)


def solution(mesh):
    split = Mesh(mesh.devices.reshape(4, 8, 4, 2), ("grp", "z", "y", "core"))
    cell = ("z", "y", "core")
    return jax.shard_map(
        on_device,
        mesh=split,
        in_specs=(P("grp", None, cell), P("grp", None, cell), P(cell, None), P()),
        out_specs=(P(None, cell), P(cell)),
        check_vma=False,
    )
```

```python
import functools

import jax
import jax.numpy as jnp
from jax import lax
from jax.experimental import pallas as pl
from jax.experimental.pallas import tpu as pltpu
from jax.sharding import Mesh, PartitionSpec as P

HIGHEST = lax.Precision.HIGHEST
F32 = jnp.float32
BF16 = jnp.bfloat16
VMEM = pl.BlockSpec(memory_space=pltpu.VMEM)
SMEM = pl.BlockSpec(memory_space=pltpu.SMEM)


def project_kernel(chunk, first_slot, halves, *refs):
    half_ref, fields_ref, scale_ref, basis_ref = refs[:4]
    refs = refs[4:]
    base_ref = None
    if first_slot:
        base_ref, refs = refs[0], refs[1:]
    outs, refs = refs[:halves], refs[halves:]
    buffer, weights, spread, scales3, sems = refs
    _, rows, slots, cells = buffer.shape
    packed = rows // 2
    modes = basis_ref.shape[0]
    lanes = 128
    blocks = cells // lanes
    chunks = packed // chunk
    groups = slots // 8
    bases = [(half_ref[0] if i == 0 else 1 - half_ref[0]) * rows for i in range(halves)]

    def fetch(part, index, which):
        first = which * packed + index * chunk
        return pltpu.make_async_copy(
            fields_ref.at[pl.ds(bases[part] + first, chunk), first_slot : first_slot + slots],
            buffer.at[part, pl.ds(first, chunk)],
            sems.at[part, index, which],
        )

    for part in range(halves):
        for index in range(chunks):
            for which in range(2):
                fetch(part, index, which).start()

    turned = basis_ref[...].astype(F32).T.astype(BF16)
    none = jnp.zeros_like(turned)
    weights[0] = jnp.concatenate([turned, none], axis=1)
    weights[1] = jnp.concatenate([none, turned], axis=1)
    block_of_row = lax.broadcasted_iota(jnp.int32, (256, lanes), 0) % blocks
    for block in range(blocks):
        spread[:, block * lanes : (block + 1) * lanes] = jnp.where(block_of_row == block, 1.0, 0.0).astype(BF16)
    by_row = scale_ref[...].T
    high = by_row.astype(BF16).astype(F32)
    rest = by_row - high
    middle = rest.astype(BF16).astype(F32)
    low = rest - middle
    lane = lax.broadcasted_iota(jnp.int32, (by_row.shape[0], 128), 1)
    group_of = [first_slot // 8 + g for g in range(groups)]
    for g, q in enumerate(group_of):
        cut = slice(q // 2 * 128, q // 2 * 128 + 128)
        turned_middle = pltpu.roll(middle[:, cut], 64, 1)
        if q % 2 == 0:
            scales3[g, :, :128] = jnp.where(lane < 64, high[:, cut], turned_middle)
        else:
            scales3[g, :, :128] = jnp.where(lane < 64, turned_middle, high[:, cut])
        scales3[g, :, 128:] = low[:, cut]

    slot8 = lax.broadcasted_iota(jnp.int32, (8, 256), 0)
    lane8 = lax.broadcasted_iota(jnp.int32, (8, 256), 1)
    own = (lane8 % 64) // 8 == slot8
    masks = (own & (lane8 < 192), own & ((lane8 < 128) | (lane8 >= 192)))
    slot = lax.broadcasted_iota(jnp.int32, (slots, 2 * modes), 0)
    for part in range(halves):
        for index in range(chunks):
            total = None
            for which in range(2):
                fetch(part, index, which).wait()
                first = which * packed + index * chunk
                left = []
                for row in range(chunk):
                    for g, q in enumerate(group_of):
                        line = jnp.broadcast_to(scales3[g, pl.ds(bases[part] + first + row, 1), :], (8, 256))
                        left.append(jnp.where(masks[q % 2], line, 0.0))
                left = jnp.concatenate(left, axis=0).astype(BF16)
                scale = jnp.dot(left, spread[...], preferred_element_type=F32)
                piece = buffer[part, first : first + chunk].astype(F32).reshape(chunk * slots, cells)
                dequant = (piece * scale).astype(BF16)
                product = jnp.dot(dequant, weights[which], preferred_element_type=F32)
                total = product if total is None else total + product
            tiles = []
            for row in range(chunk):
                tile = total[row * slots : (row + 1) * slots]
                if base_ref is None:
                    tile = tile - jnp.where(slot >= 2, jnp.broadcast_to(tile[:1], tile.shape), 0.0)
                else:
                    line = base_ref[0, index * chunk + row : index * chunk + row + 1, :]
                    tile = tile - jnp.broadcast_to(line, tile.shape)
                tiles.append(tile)
            outs[part][:, index * chunk : (index + 1) * chunk, :] = jnp.swapaxes(jnp.stack(tiles), 0, 1)

def project(half, fields, scales, basis, base=None):
    rows, slots, cells = fields.shape
    modes = basis.shape[0]
    packed = rows // 4
    first_slot, count, halves = (0, 8, 2) if base is None else (8, slots - 8, 1)
    chunk = 16 if base is None else 8
    chunks = packed // chunk
    out = jax.ShapeDtypeStruct((count, packed, 2 * modes), F32)
    extra = [] if base is None else [base]
    return pl.pallas_call(
        functools.partial(project_kernel, chunk, first_slot, halves),
        in_specs=[SMEM, pl.BlockSpec(memory_space=pl.ANY), VMEM, VMEM] + [VMEM] * len(extra),
        out_specs=[VMEM] * halves,
        out_shape=[out] * halves,
        scratch_shapes=[
            pltpu.VMEM((halves, rows // 2, count, cells), BF16),
            pltpu.VMEM((2, cells, 2 * modes), BF16),
            pltpu.VMEM((256, cells), BF16),
            pltpu.VMEM((count // 8, rows, 256), F32),
            pltpu.SemaphoreType.DMA((halves, chunks, 2)),
        ],
        compiler_params=pltpu.CompilerParams(vmem_limit_bytes=52 << 20),
        cost_estimate=pl.CostEstimate(
            flops=halves * rows * count * cells * modes, bytes_accessed=halves * rows * count * cells, transcendentals=0
        ),
        name="first" if base is None else "rest",
    )(half, fields, scales, basis, *extra)


def moments_kernel(where_ref, parts_ref, second_ref, keep_ref, send_ref):
    slot, half = where_ref[0], where_ref[1]
    own = parts_ref[0]
    for source in range(1, parts_ref.shape[0]):
        own = own + parts_ref[source]
    second = second_ref[0]
    for source in range(1, second_ref.shape[0]):
        second = second + second_ref[source]
    left = jnp.where(slot == 0, own, second)
    wide = lax.dot_general(left, own, (((0,), (0,)), ((), ())), precision=HIGHEST, preferred_element_type=F32)
    matrix = wide[:64, :64] + wide[64:, 64:]
    sums = jnp.sum(own, axis=0, keepdims=True)
    sums = sums[:, :64] + sums[:, 64:]
    low = jnp.concatenate([sums[:, 32:], sums[:, :32]], axis=1)
    row = lax.broadcasted_iota(jnp.int32, matrix.shape, 0)
    lane = lax.broadcasted_iota(jnp.int32, matrix.shape, 1)
    spare = (slot < 2) & (lane < 32)
    matrix = jnp.where(spare & (row == 32), jnp.broadcast_to(sums, matrix.shape), matrix)
    matrix = jnp.where(spare & (row == 33), jnp.broadcast_to(low, matrix.shape), matrix)
    upper = jnp.concatenate([matrix[:16], matrix[16:32]], axis=1)
    lower = jnp.concatenate([matrix[32:48], matrix[48:]], axis=1)
    keep_ref[...] = jnp.where(half == 0, upper, lower)
    send_ref[...] = jnp.where(half == 0, lower, upper)


def moments(where, parts, second):
    out = jax.ShapeDtypeStruct((16, 128), F32)
    return pl.pallas_call(
        moments_kernel,
        in_specs=[SMEM, VMEM, VMEM],
        out_specs=(VMEM, VMEM),
        out_shape=(out, out),
        compiler_params=pltpu.CompilerParams(vmem_limit_bytes=16 << 20),
        cost_estimate=pl.CostEstimate(flops=1 << 22, bytes_accessed=1 << 20, transcendentals=0),
        name="moments",
    )(where, parts, second)


def three(value):
    high = value.astype(BF16)
    rest = value - high.astype(F32)
    middle = rest.astype(BF16)
    return high, middle, (rest - middle.astype(F32)).astype(BF16)


def maps_kernel(rows_total, cell_total, half_ref, order_ref, mine_ref, other_ref, basis_ref, maps_ref, total_ref):
    half = half_ref[0]
    mine, other = mine_ref[...], other_ref[...]
    halves = (jnp.where(half == 0, mine, other), jnp.where(half == 0, other, mine))
    slots = mine.shape[0]
    modes, cells = basis_ref.shape
    phi = basis_ref[...]
    none = jnp.zeros_like(phi)
    right_first = jnp.concatenate([phi, phi, phi, none], axis=0)
    right_second = jnp.concatenate([phi, phi, none, phi], axis=0)
    phi32 = phi.astype(F32)

    def quadratic(pieces):
        count = pieces[0].shape[0]
        result = None
        for part, piece in enumerate(pieces):
            flat = piece.reshape(count * 16, 128)
            lane = lax.broadcasted_iota(jnp.int32, flat.shape, 1)
            high = flat.astype(BF16).astype(F32)
            rest = flat - high
            middle = rest.astype(BF16).astype(F32)
            low = (rest - middle).astype(BF16)
            turned = pltpu.roll(middle, 64, 1)
            for side, right in enumerate((right_first, right_second)):
                front = jnp.where((lane < 64) == (side == 0), high, turned).astype(BF16)
                left = jnp.concatenate([front, low], axis=1)
                product = jnp.dot(left, right, preferred_element_type=F32).reshape(count, 16, cells)
                first = 32 * part + 16 * side
                term = jnp.sum(product * phi32[None, first : first + 16], axis=1)
                result = term if result is None else result + term
        return result

    group = 8
    for start in range(0, slots, group):
        found = cell_total / rows_total * quadratic([h[start : start + group] for h in halves])
        for slot in range(max(start, 2), start + group):
            maps_ref[pl.ds(order_ref[slot - 2], 1), :] = found[slot - start : slot - start + 1]

    both = [h[0] + h[1] for h in halves]
    sums = both[1][0:1, :64]
    low = both[1][1:2, :64]
    lane1 = lax.broadcasted_iota(jnp.int32, sums.shape, 1)
    sums = jnp.where(lane1 < 32, sums, jnp.concatenate([low[:, 32:], low[:, :32]], axis=1))
    average = sums / (2.0 * rows_total)
    outer = lax.dot_general(average, average, (((0,), (0,)), ((), ())), precision=HIGHEST, preferred_element_type=F32)
    lane = lax.broadcasted_iota(jnp.int32, both[0].shape, 1)
    column = jnp.where(lane < 64, lane, lane - 64)
    weight = jnp.where(column < 32, 1.0, 2.0)
    outer_upper = jnp.concatenate([outer[:16], outer[16:32]], axis=1)
    outer_lower = jnp.concatenate([outer[32:48], outer[48:]], axis=1)
    upper = (both[0] / (2.0 * rows_total) - outer_upper) * weight
    lower = jnp.where(column < 32, 0.0, both[1] / (2.0 * rows_total) - outer_lower)
    total = quadratic([upper[None], lower[None]])
    total_ref[...] = cell_total * total


def make_maps(rows_total, cell_total, half, order, mine, other, basis):
    cells = basis.shape[1]
    params = order.shape[0]

    def kernel(*refs):
        maps_kernel(rows_total, cell_total, *refs)

    return pl.pallas_call(
        kernel,
        in_specs=[SMEM, SMEM, VMEM, VMEM, VMEM],
        out_specs=(VMEM, VMEM),
        out_shape=(jax.ShapeDtypeStruct((params, cells), F32), jax.ShapeDtypeStruct((1, cells), F32)),
        compiler_params=pltpu.CompilerParams(vmem_limit_bytes=32 << 20),
        cost_estimate=pl.CostEstimate(flops=1 << 28, bytes_accessed=1 << 20, transcendentals=0),
        name="maps",
    )(half, order, mine, other, basis)


def shifted(value, axis, size, shift):
    return lax.ppermute(value, axis, [(i, (i + shift) % size) for i in range(size)])


def on_device(fields, scales, pod_basis, param_order):
    rows, slots, cells = fields.shape
    blocks = scales.shape[2]
    modes = pod_basis.shape[1]
    sizes = {name: lax.axis_size(name) for name in ("grp", "z", "y", "core")}
    rows_total = float(rows * sizes["grp"])
    cell_total = float(cells * sizes["z"] * sizes["y"] * sizes["core"])
    core = lax.axis_index("core").astype(jnp.int32)
    slot = (lax.axis_index("z") * sizes["y"] + lax.axis_index("y")).astype(jnp.int32)
    by_slot = jnp.transpose(scales, (1, 2, 0)).reshape(slots * blocks, rows)
    basis = pod_basis.T
    packed = rows // 4

    theirs_first, ours_first = project((1 - core)[None], fields, by_slot, basis)
    near_first = ours_first + shifted(theirs_first, "core", 2, 1)
    (theirs_rest,) = project((1 - core)[None], fields, by_slot, basis, theirs_first)
    second = near_first[1]
    second = second + sum(shifted(second, "y", sizes["y"], s) for s in range(1, sizes["y"]))
    got_rest = shifted(theirs_rest, "core", 2, 1)
    (ours_rest,) = project(core[None], fields, by_slot, basis, ours_first)
    halves = jnp.concatenate([near_first, ours_rest + got_rest], axis=0)
    halves, second = lax.optimization_barrier((halves, second))
    parts = lax.all_to_all(halves, ("z", "y"), 0, 0, tiled=True)
    second = second + sum(shifted(second, "z", sizes["z"], s) for s in range(1, sizes["z"] // 2))
    second = jnp.stack([second, shifted(second, "z", sizes["z"], sizes["z"] // 2)])

    keep, send = moments(jnp.stack([slot, core]), parts, second)
    piece = keep + shifted(send, "core", 2, 1)
    piece = piece + sum(shifted(piece, "grp", sizes["grp"], s) for s in range(1, sizes["grp"]))
    copies = jnp.broadcast_to(piece[None], (slots,) + piece.shape)
    mine = lax.all_to_all(copies, ("z", "y"), 0, 0, tiled=True)
    other = shifted(mine, "core", 2, 1)
    sobol, total = make_maps(rows_total, cell_total, core[None], param_order, mine, other, basis)
    return sobol, total.reshape(cells)


def solution(mesh):
    split = Mesh(mesh.devices.reshape(4, 8, 4, 2), ("grp", "z", "y", "core"))
    cell = ("z", "y", "core")
    return jax.shard_map(
        on_device,
        mesh=split,
        in_specs=(P("grp", None, cell), P("grp", None, cell), P(cell, None), P()),
        out_specs=(P(None, cell), P(cell)),
        check_vma=False,
    )
```

```python
import functools

import jax
import jax.numpy as jnp
from jax import lax
from jax.experimental import pallas as pl
from jax.experimental.pallas import tpu as pltpu
from jax.sharding import Mesh, PartitionSpec as P

HIGHEST = lax.Precision.HIGHEST
F32 = jnp.float32
BF16 = jnp.bfloat16
VMEM = pl.BlockSpec(memory_space=pltpu.VMEM)
SMEM = pl.BlockSpec(memory_space=pltpu.SMEM)


def project_kernel(chunk, where_ref, fields_ref, scale_ref, basis_ref, out_ref, buffer, weights, spread, scales3, sems):
    rows, slots, cells = buffer.shape
    packed = rows // 2
    modes = basis_ref.shape[0]
    lanes = 128
    blocks = cells // lanes
    chunks = packed // chunk
    groups = slots // 8
    base = where_ref[0] * rows

    def fetch(index, which):
        first = which * packed + index * chunk
        return pltpu.make_async_copy(
            fields_ref.at[pl.ds(base + first, chunk)], buffer.at[pl.ds(first, chunk)], sems.at[index, which]
        )

    for index in range(chunks):
        for which in range(2):
            fetch(index, which).start()

    turned = basis_ref[...].astype(F32).T.astype(BF16)
    none = jnp.zeros_like(turned)
    weights[0] = jnp.concatenate([turned, none], axis=1)
    weights[1] = jnp.concatenate([none, turned], axis=1)
    block_of_row = lax.broadcasted_iota(jnp.int32, (256, lanes), 0) % blocks
    for block in range(blocks):
        spread[:, block * lanes : (block + 1) * lanes] = jnp.where(block_of_row == block, 1.0, 0.0).astype(BF16)
    by_row = scale_ref[...].T
    high = by_row.astype(BF16).astype(F32)
    rest = by_row - high
    middle = rest.astype(BF16).astype(F32)
    low = rest - middle
    lane = lax.broadcasted_iota(jnp.int32, (by_row.shape[0], 128), 1)
    for q in range(groups):
        cut = slice(q // 2 * 128, q // 2 * 128 + 128)
        turned_middle = pltpu.roll(middle[:, cut], 64, 1)
        if q % 2 == 0:
            scales3[q, :, :128] = jnp.where(lane < 64, high[:, cut], turned_middle)
        else:
            scales3[q, :, :128] = jnp.where(lane < 64, turned_middle, high[:, cut])
        scales3[q, :, 128:] = low[:, cut]

    slot8 = lax.broadcasted_iota(jnp.int32, (8, 256), 0)
    lane8 = lax.broadcasted_iota(jnp.int32, (8, 256), 1)
    own = (lane8 % 64) // 8 == slot8
    masks = (own & (lane8 < 192), own & ((lane8 < 128) | (lane8 >= 192)))
    slot = lax.broadcasted_iota(jnp.int32, (slots, 2 * modes), 0)
    for index in range(chunks):
        total = None
        for which in range(2):
            fetch(index, which).wait()
            first = which * packed + index * chunk
            left = []
            for row in range(chunk):
                for q in range(groups):
                    line = jnp.broadcast_to(scales3[q, pl.ds(base + first + row, 1), :], (8, 256))
                    left.append(jnp.where(masks[q % 2], line, 0.0))
            left = jnp.concatenate(left, axis=0).astype(BF16)
            scale = jnp.dot(left, spread[...], preferred_element_type=F32)
            piece = buffer[first : first + chunk].astype(F32).reshape(chunk * slots, cells)
            dequant = (piece * scale).astype(BF16)
            product = jnp.dot(dequant, weights[which], preferred_element_type=F32)
            total = product if total is None else total + product
        tiles = []
        for row in range(chunk):
            tile = total[row * slots : (row + 1) * slots]
            tiles.append(tile - jnp.where(slot >= 2, jnp.broadcast_to(tile[:1], tile.shape), 0.0))
        turned = jnp.swapaxes(jnp.stack(tiles), 0, 1)
        for group in range(4):
            place = lax.rem(group + 4 - where_ref[1], 4)
            out_ref[place, :, index * chunk : (index + 1) * chunk, :] = turned[8 * group : 8 * group + 8]

def project(where, fields, scales, basis):
    rows, slots, cells = fields.shape
    modes = basis.shape[0]
    packed = rows // 4
    chunk = 8
    chunks = packed // chunk
    return pl.pallas_call(
        functools.partial(project_kernel, chunk),
        in_specs=[SMEM, pl.BlockSpec(memory_space=pl.ANY), VMEM, VMEM],
        out_specs=VMEM,
        out_shape=jax.ShapeDtypeStruct((4, slots // 4, packed, 2 * modes), F32),
        scratch_shapes=[
            pltpu.VMEM((rows // 2, slots, cells), BF16),
            pltpu.VMEM((2, cells, 2 * modes), BF16),
            pltpu.VMEM((256, cells), BF16),
            pltpu.VMEM((slots // 8, rows, 256), F32),
            pltpu.SemaphoreType.DMA((chunks, 2)),
        ],
        compiler_params=pltpu.CompilerParams(vmem_limit_bytes=52 << 20),
        cost_estimate=pl.CostEstimate(
            flops=rows * slots * cells * modes, bytes_accessed=rows * slots * cells, transcendentals=0
        ),
        name="project",
    )(where, fields, scales, basis)


def combine_kernel(where_ref, ours_ref, got_ref, *outs):
    place = lax.rem(4 - where_ref[1], 4)
    second = ours_ref[place, 1] + got_ref[place, 1]
    for group, out in enumerate(outs):
        out[:8] = ours_ref[group] + got_ref[group]
        out[8] = second


def combine(where, ours, got):
    groups, count, packed, lanes = ours.shape
    out = jax.ShapeDtypeStruct((count + 1, packed, lanes), F32)
    return pl.pallas_call(
        combine_kernel,
        in_specs=[SMEM, VMEM, VMEM],
        out_specs=[VMEM] * groups,
        out_shape=[out] * groups,
        compiler_params=pltpu.CompilerParams(vmem_limit_bytes=16 << 20),
        cost_estimate=pl.CostEstimate(flops=1 << 18, bytes_accessed=1 << 21, transcendentals=0),
        name="combine",
    )(where, ours, got)


def add_up_kernel(*refs):
    *parts, out_ref = refs
    total = parts[0][...]
    for part in parts[1:]:
        total = total + part[...]
    packed = total.shape[1]
    out_ref[:, :packed] = total[:8]
    out_ref[:, packed:] = jnp.broadcast_to(total[8:], total[:8].shape)


def add_up(parts):
    count, packed, lanes = parts[0].shape
    return pl.pallas_call(
        add_up_kernel,
        in_specs=[VMEM] * len(parts),
        out_specs=VMEM,
        out_shape=jax.ShapeDtypeStruct((count - 1, 2 * packed, lanes), F32),
        compiler_params=pltpu.CompilerParams(vmem_limit_bytes=16 << 20),
        cost_estimate=pl.CostEstimate(flops=1 << 18, bytes_accessed=1 << 20, transcendentals=0),
        name="add_up",
    )(*parts)


def moments_kernel(where_ref, parts_ref, keep_ref, send_ref):
    slot, half = where_ref[0], where_ref[1]
    both = parts_ref[0]
    for source in range(1, parts_ref.shape[0]):
        both = both + parts_ref[source]
    own, second = both[:32], both[32:]
    left = jnp.where(slot == 0, own, second)
    wide = lax.dot_general(left, own, (((0,), (0,)), ((), ())), precision=HIGHEST, preferred_element_type=F32)
    matrix = wide[:64, :64] + wide[64:, 64:]
    sums = jnp.sum(own, axis=0, keepdims=True)
    sums = sums[:, :64] + sums[:, 64:]
    low = jnp.concatenate([sums[:, 32:], sums[:, :32]], axis=1)
    row = lax.broadcasted_iota(jnp.int32, matrix.shape, 0)
    lane = lax.broadcasted_iota(jnp.int32, matrix.shape, 1)
    spare = (slot < 2) & (lane < 32)
    matrix = jnp.where(spare & (row == 32), jnp.broadcast_to(sums, matrix.shape), matrix)
    matrix = jnp.where(spare & (row == 33), jnp.broadcast_to(low, matrix.shape), matrix)
    upper = jnp.concatenate([matrix[:16], matrix[16:32]], axis=1)
    lower = jnp.concatenate([matrix[32:48], matrix[48:]], axis=1)
    keep_ref[...] = jnp.where(half == 0, upper, lower)
    send_ref[...] = jnp.where(half == 0, lower, upper)


def moments(where, parts):
    out = jax.ShapeDtypeStruct((16, 128), F32)
    return pl.pallas_call(
        moments_kernel,
        in_specs=[SMEM, VMEM],
        out_specs=(VMEM, VMEM),
        out_shape=(out, out),
        compiler_params=pltpu.CompilerParams(vmem_limit_bytes=16 << 20),
        cost_estimate=pl.CostEstimate(flops=1 << 22, bytes_accessed=1 << 20, transcendentals=0),
        name="moments",
    )(where, parts)


def three(value):
    high = value.astype(BF16)
    rest = value - high.astype(F32)
    middle = rest.astype(BF16)
    return high, middle, (rest - middle.astype(F32)).astype(BF16)


def maps_kernel(rows_total, cell_total, half_ref, order_ref, mine_ref, other_ref, basis_ref, maps_ref, total_ref):
    half = half_ref[0]
    mine, other = mine_ref[...], other_ref[...]
    halves = (jnp.where(half == 0, mine, other), jnp.where(half == 0, other, mine))
    slots = mine.shape[0]
    modes, cells = basis_ref.shape
    phi = basis_ref[...]
    none = jnp.zeros_like(phi)
    right_first = jnp.concatenate([phi, phi, phi, none], axis=0)
    right_second = jnp.concatenate([phi, phi, none, phi], axis=0)
    phi32 = phi.astype(F32)

    def quadratic(pieces):
        count = pieces[0].shape[0]
        result = None
        for part, piece in enumerate(pieces):
            flat = piece.reshape(count * 16, 128)
            lane = lax.broadcasted_iota(jnp.int32, flat.shape, 1)
            high = flat.astype(BF16).astype(F32)
            rest = flat - high
            middle = rest.astype(BF16).astype(F32)
            low = (rest - middle).astype(BF16)
            turned = pltpu.roll(middle, 64, 1)
            for side, right in enumerate((right_first, right_second)):
                front = jnp.where((lane < 64) == (side == 0), high, turned).astype(BF16)
                left = jnp.concatenate([front, low], axis=1)
                product = jnp.dot(left, right, preferred_element_type=F32).reshape(count, 16, cells)
                first = 32 * part + 16 * side
                term = jnp.sum(product * phi32[None, first : first + 16], axis=1)
                result = term if result is None else result + term
        return result

    group = 8
    for start in range(0, slots, group):
        found = cell_total / rows_total * quadratic([h[start : start + group] for h in halves])
        for slot in range(max(start, 2), start + group):
            maps_ref[pl.ds(order_ref[slot - 2], 1), :] = found[slot - start : slot - start + 1]

    both = [h[0] + h[1] for h in halves]
    sums = both[1][0:1, :64]
    low = both[1][1:2, :64]
    lane1 = lax.broadcasted_iota(jnp.int32, sums.shape, 1)
    sums = jnp.where(lane1 < 32, sums, jnp.concatenate([low[:, 32:], low[:, :32]], axis=1))
    average = sums / (2.0 * rows_total)
    outer = lax.dot_general(average, average, (((0,), (0,)), ((), ())), precision=HIGHEST, preferred_element_type=F32)
    lane = lax.broadcasted_iota(jnp.int32, both[0].shape, 1)
    column = jnp.where(lane < 64, lane, lane - 64)
    weight = jnp.where(column < 32, 1.0, 2.0)
    outer_upper = jnp.concatenate([outer[:16], outer[16:32]], axis=1)
    outer_lower = jnp.concatenate([outer[32:48], outer[48:]], axis=1)
    upper = (both[0] / (2.0 * rows_total) - outer_upper) * weight
    lower = jnp.where(column < 32, 0.0, both[1] / (2.0 * rows_total) - outer_lower)
    total = quadratic([upper[None], lower[None]])
    total_ref[...] = cell_total * total


def make_maps(rows_total, cell_total, half, order, mine, other, basis):
    cells = basis.shape[1]
    params = order.shape[0]

    def kernel(*refs):
        maps_kernel(rows_total, cell_total, *refs)

    return pl.pallas_call(
        kernel,
        in_specs=[SMEM, SMEM, VMEM, VMEM, VMEM],
        out_specs=(VMEM, VMEM),
        out_shape=(jax.ShapeDtypeStruct((params, cells), F32), jax.ShapeDtypeStruct((1, cells), F32)),
        compiler_params=pltpu.CompilerParams(vmem_limit_bytes=32 << 20),
        cost_estimate=pl.CostEstimate(flops=1 << 28, bytes_accessed=1 << 20, transcendentals=0),
        name="maps",
    )(half, order, mine, other, basis)


def shifted(value, axis, size, shift):
    return lax.ppermute(value, axis, [(i, (i + shift) % size) for i in range(size)])


def on_device(fields, scales, pod_basis, param_order):
    rows, slots, cells = fields.shape
    blocks = scales.shape[2]
    modes = pod_basis.shape[1]
    sizes = {name: lax.axis_size(name) for name in ("grp", "z", "y", "core")}
    rows_total = float(rows * sizes["grp"])
    cell_total = float(cells * sizes["z"] * sizes["y"] * sizes["core"])
    core = lax.axis_index("core").astype(jnp.int32)
    slot = (lax.axis_index("y") * sizes["z"] + lax.axis_index("z")).astype(jnp.int32)
    by_slot = jnp.transpose(scales, (1, 2, 0)).reshape(slots * blocks, rows)
    basis = pod_basis.T

    height = lax.axis_index("y").astype(jnp.int32)
    theirs = project(jnp.stack([1 - core, height]), fields, by_slot, basis)
    got = shifted(theirs, "core", 2, 1)
    where = jnp.stack([core, height])
    ours = project(where, fields, by_slot, basis)
    pieces = combine(where, ours, got)
    parts = add_up([pieces[0]] + [shifted(pieces[s], "y", sizes["y"], s) for s in range(1, sizes["y"])])
    parts = lax.all_to_all(parts, "z", 0, 0, tiled=True)

    keep, send = moments(jnp.stack([slot, core]), parts)
    piece = keep + shifted(send, "core", 2, 1)
    piece = piece + sum(shifted(piece, "grp", sizes["grp"], s) for s in range(1, sizes["grp"]))
    copies = jnp.broadcast_to(piece[None], (slots,) + piece.shape)
    mine = lax.all_to_all(copies, ("y", "z"), 0, 0, tiled=True)
    other = shifted(mine, "core", 2, 1)
    sobol, total = make_maps(rows_total, cell_total, core[None], param_order, mine, other, basis)
    return sobol, total.reshape(cells)


def solution(mesh):
    split = Mesh(mesh.devices.reshape(4, 8, 4, 2), ("grp", "z", "y", "core"))
    cell = ("z", "y", "core")
    return jax.shard_map(
        on_device,
        mesh=split,
        in_specs=(P("grp", None, cell), P("grp", None, cell), P(cell, None), P()),
        out_specs=(P(None, cell), P(cell)),
        check_vma=False,
    )
```

```python
import functools

import jax
import jax.numpy as jnp
from jax import lax
from jax.experimental import pallas as pl
from jax.experimental.pallas import tpu as pltpu
from jax.sharding import Mesh, PartitionSpec as P

HIGHEST = lax.Precision.HIGHEST
F32 = jnp.float32
BF16 = jnp.bfloat16
VMEM = pl.BlockSpec(memory_space=pltpu.VMEM)
SMEM = pl.BlockSpec(memory_space=pltpu.SMEM)


def project_kernel(chunk, where_ref, fields_ref, scale_ref, basis_ref, out_ref, buffer, weights, spread, scales3, sems):
    rows, slots, cells = buffer.shape
    packed = rows // 2
    modes = basis_ref.shape[0]
    lanes = 128
    blocks = cells // lanes
    chunks = packed // chunk
    groups = slots // 8
    base = where_ref[0] * rows

    def fetch(index, which):
        first = which * packed + index * chunk
        return pltpu.make_async_copy(
            fields_ref.at[pl.ds(base + first, chunk)], buffer.at[pl.ds(first, chunk)], sems.at[index, which]
        )

    for index in range(chunks):
        for which in range(2):
            fetch(index, which).start()

    weights[...] = basis_ref[...].astype(F32).T.astype(BF16)
    block_of_row = lax.broadcasted_iota(jnp.int32, (256, lanes), 0) % blocks
    for block in range(blocks):
        spread[:, block * lanes : (block + 1) * lanes] = jnp.where(block_of_row == block, 1.0, 0.0).astype(BF16)
    by_row = scale_ref[...].T
    high = by_row.astype(BF16).astype(F32)
    rest = by_row - high
    middle = rest.astype(BF16).astype(F32)
    low = rest - middle
    lane = lax.broadcasted_iota(jnp.int32, (by_row.shape[0], 128), 1)
    for q in range(groups):
        cut = slice(q // 2 * 128, q // 2 * 128 + 128)
        turned_middle = pltpu.roll(middle[:, cut], 64, 1)
        if q % 2 == 0:
            scales3[q, :, :128] = jnp.where(lane < 64, high[:, cut], turned_middle)
        else:
            scales3[q, :, :128] = jnp.where(lane < 64, turned_middle, high[:, cut])
        scales3[q, :, 128:] = low[:, cut]

    slot8 = lax.broadcasted_iota(jnp.int32, (8, 256), 0)
    lane8 = lax.broadcasted_iota(jnp.int32, (8, 256), 1)
    own = (lane8 % 64) // 8 == slot8
    masks = (own & (lane8 < 192), own & ((lane8 < 128) | (lane8 >= 192)))
    slot = lax.broadcasted_iota(jnp.int32, (slots, 2 * modes), 0)
    for index in range(chunks):
        left, pieces = [], []
        for which in range(2):
            fetch(index, which).wait()
            first = which * packed + index * chunk
            for row in range(chunk):
                for q in range(groups):
                    line = jnp.broadcast_to(scales3[q, pl.ds(base + first + row, 1), :], (8, 256))
                    left.append(jnp.where(masks[q % 2], line, 0.0))
            pieces.append(buffer[first : first + chunk].astype(F32).reshape(chunk * slots, cells))
        left = jnp.concatenate(left, axis=0).astype(BF16)
        scale = jnp.dot(left, spread[...], preferred_element_type=F32)
        dequant = (jnp.concatenate(pieces, axis=0) * scale).astype(BF16)
        product = jnp.dot(dequant, weights[...], preferred_element_type=F32)
        total = jnp.concatenate([product[: chunk * slots], product[chunk * slots :]], axis=1)
        tiles = []
        for row in range(chunk):
            tile = total[row * slots : (row + 1) * slots]
            tiles.append(tile - jnp.where(slot >= 2, jnp.broadcast_to(tile[:1], tile.shape), 0.0))
        turned = jnp.swapaxes(jnp.stack(tiles), 0, 1)
        for group in range(4):
            place = lax.rem(group + 4 - where_ref[1], 4)
            out_ref[place, :, index * chunk : (index + 1) * chunk, :] = turned[8 * group : 8 * group + 8]

def project(where, fields, scales, basis, room=52):
    rows, slots, cells = fields.shape
    modes = basis.shape[0]
    packed = rows // 4
    chunk = 16
    chunks = packed // chunk
    return pl.pallas_call(
        functools.partial(project_kernel, chunk),
        in_specs=[SMEM, pl.BlockSpec(memory_space=pl.ANY), VMEM, VMEM],
        out_specs=VMEM,
        out_shape=jax.ShapeDtypeStruct((4, slots // 4, packed, 2 * modes), F32),
        scratch_shapes=[
            pltpu.VMEM((rows // 2, slots, cells), BF16),
            pltpu.VMEM((cells, modes), BF16),
            pltpu.VMEM((256, cells), BF16),
            pltpu.VMEM((slots // 8, rows, 256), F32),
            pltpu.SemaphoreType.DMA((chunks, 2)),
        ],
        compiler_params=pltpu.CompilerParams(vmem_limit_bytes=room << 20),
        cost_estimate=pl.CostEstimate(
            flops=rows * slots * cells * modes, bytes_accessed=rows * slots * cells, transcendentals=0
        ),
        name="project",
    )(where, fields, scales, basis)


def combine_kernel(where_ref, ours_ref, got_ref, *outs):
    place = lax.rem(4 - where_ref[1], 4)
    second = ours_ref[place, 1] + got_ref[place, 1]
    for group, out in enumerate(outs):
        out[:8] = ours_ref[group] + got_ref[group]
        out[8] = second


def combine(where, ours, got):
    groups, count, packed, lanes = ours.shape
    out = jax.ShapeDtypeStruct((count + 1, packed, lanes), F32)
    return pl.pallas_call(
        combine_kernel,
        in_specs=[SMEM, VMEM, VMEM],
        out_specs=[VMEM] * groups,
        out_shape=[out] * groups,
        compiler_params=pltpu.CompilerParams(vmem_limit_bytes=16 << 20),
        cost_estimate=pl.CostEstimate(flops=1 << 18, bytes_accessed=1 << 21, transcendentals=0),
        name="combine",
    )(where, ours, got)


def add_up_kernel(*refs):
    *parts, out_ref = refs
    total = parts[0][...]
    for part in parts[1:]:
        total = total + part[...]
    packed = total.shape[1]
    out_ref[:, :packed] = total[:8]
    out_ref[:, packed:] = jnp.broadcast_to(total[8:], total[:8].shape)


def add_up(parts):
    count, packed, lanes = parts[0].shape
    return pl.pallas_call(
        add_up_kernel,
        in_specs=[VMEM] * len(parts),
        out_specs=VMEM,
        out_shape=jax.ShapeDtypeStruct((count - 1, 2 * packed, lanes), F32),
        compiler_params=pltpu.CompilerParams(vmem_limit_bytes=16 << 20),
        cost_estimate=pl.CostEstimate(flops=1 << 18, bytes_accessed=1 << 20, transcendentals=0),
        name="add_up",
    )(*parts)


def moments_kernel(where_ref, parts_ref, keep_ref, send_ref):
    slot, half = where_ref[0], where_ref[1]
    both = parts_ref[0]
    for source in range(1, parts_ref.shape[0]):
        both = both + parts_ref[source]
    own, second = both[:32], both[32:]
    left = jnp.where(slot == 0, own, second)
    wide = lax.dot_general(left, own, (((0,), (0,)), ((), ())), precision=HIGHEST, preferred_element_type=F32)
    matrix = wide[:64, :64] + wide[64:, 64:]
    sums = jnp.sum(own, axis=0, keepdims=True)
    sums = sums[:, :64] + sums[:, 64:]
    low = jnp.concatenate([sums[:, 32:], sums[:, :32]], axis=1)
    row = lax.broadcasted_iota(jnp.int32, matrix.shape, 0)
    lane = lax.broadcasted_iota(jnp.int32, matrix.shape, 1)
    spare = (slot < 2) & (lane < 32)
    matrix = jnp.where(spare & (row == 32), jnp.broadcast_to(sums, matrix.shape), matrix)
    matrix = jnp.where(spare & (row == 33), jnp.broadcast_to(low, matrix.shape), matrix)
    upper = jnp.concatenate([matrix[:16], matrix[16:32]], axis=1)
    lower = jnp.concatenate([matrix[32:48], matrix[48:]], axis=1)
    keep_ref[...] = jnp.where(half == 0, upper, lower)
    send_ref[...] = jnp.where(half == 0, lower, upper)


def moments(where, parts):
    out = jax.ShapeDtypeStruct((16, 128), F32)
    return pl.pallas_call(
        moments_kernel,
        in_specs=[SMEM, VMEM],
        out_specs=(VMEM, VMEM),
        out_shape=(out, out),
        compiler_params=pltpu.CompilerParams(vmem_limit_bytes=16 << 20),
        cost_estimate=pl.CostEstimate(flops=1 << 22, bytes_accessed=1 << 20, transcendentals=0),
        name="moments",
    )(where, parts)


def three(value):
    high = value.astype(BF16)
    rest = value - high.astype(F32)
    middle = rest.astype(BF16)
    return high, middle, (rest - middle.astype(F32)).astype(BF16)


def right_sides(phi):
    none = jnp.zeros_like(phi)
    return (
        jnp.concatenate([phi, phi, phi, none], axis=0),
        jnp.concatenate([phi, phi, none, phi], axis=0),
    )


def quadratic(piece, rights, rows):
    count = piece.shape[0]
    cells = rights[0].shape[1]
    flat = piece.reshape(count * 16, 128)
    lane = lax.broadcasted_iota(jnp.int32, flat.shape, 1)
    high = flat.astype(BF16).astype(F32)
    rest = flat - high
    middle = rest.astype(BF16).astype(F32)
    low = (rest - middle).astype(BF16)
    turned = pltpu.roll(middle, 64, 1)
    result = None
    for side, right in enumerate(rights):
        front = jnp.where((lane < 64) == (side == 0), high, turned).astype(BF16)
        left = jnp.concatenate([front, low], axis=1)
        product = jnp.dot(left, right, preferred_element_type=F32).reshape(count, 16, cells)
        term = jnp.sum(product * rows[side][None], axis=1)
        result = term if result is None else result + term
    return result


def half_rows(phi32, second):
    return [
        jnp.where(second, phi32[32 + 16 * side : 48 + 16 * side], phi32[16 * side : 16 + 16 * side])
        for side in range(2)
    ]


def own_maps_kernel(half_ref, mine_ref, basis_ref, out_ref):
    rights = right_sides(basis_ref[...])
    rows = half_rows(basis_ref[...].astype(F32), half_ref[0] == 1)
    for start in range(0, out_ref.shape[0], 8):
        out_ref[start : start + 8] = quadratic(mine_ref[start : start + 8], rights, rows)


def own_maps(half, mine, basis):
    return pl.pallas_call(
        own_maps_kernel,
        in_specs=[SMEM, VMEM, VMEM],
        out_specs=VMEM,
        out_shape=jax.ShapeDtypeStruct((mine.shape[0], basis.shape[1]), F32),
        compiler_params=pltpu.CompilerParams(vmem_limit_bytes=32 << 20),
        cost_estimate=pl.CostEstimate(flops=1 << 28, bytes_accessed=1 << 20, transcendentals=0),
        name="own_maps",
    )(half, mine, basis)


def maps_kernel(rows_total, cell_total, half_ref, order_ref, own_ref, mine_ref, other_ref, basis_ref, maps_ref, total_ref):
    half = half_ref[0]
    rights = right_sides(basis_ref[...])
    phi32 = basis_ref[...].astype(F32)
    rows = half_rows(phi32, half == 0)
    slots = other_ref.shape[0]
    for start in range(0, slots, 8):
        found = own_ref[start : start + 8] + quadratic(other_ref[start : start + 8], rights, rows)
        found = cell_total / rows_total * found
        for slot in range(max(start, 2), start + 8):
            maps_ref[pl.ds(order_ref[slot - 2], 1), :] = found[slot - start : slot - start + 1]

    mine = mine_ref[0] + mine_ref[1]
    other = other_ref[0] + other_ref[1]
    upper, lower = jnp.where(half == 0, mine, other), jnp.where(half == 0, other, mine)
    sums = lower[0:1, :64]
    low = lower[1:2, :64]
    lane1 = lax.broadcasted_iota(jnp.int32, sums.shape, 1)
    sums = jnp.where(lane1 < 32, sums, jnp.concatenate([low[:, 32:], low[:, :32]], axis=1))
    average = sums / (2.0 * rows_total)
    outer = lax.dot_general(average, average, (((0,), (0,)), ((), ())), precision=HIGHEST, preferred_element_type=F32)
    lane = lax.broadcasted_iota(jnp.int32, upper.shape, 1)
    column = jnp.where(lane < 64, lane, lane - 64)
    weight = jnp.where(column < 32, 1.0, 2.0)
    outer_upper = jnp.concatenate([outer[:16], outer[16:32]], axis=1)
    outer_lower = jnp.concatenate([outer[32:48], outer[48:]], axis=1)
    upper = (upper / (2.0 * rows_total) - outer_upper) * weight
    lower = jnp.where(column < 32, 0.0, lower / (2.0 * rows_total) - outer_lower)
    total = quadratic(upper[None], rights, [phi32[:16], phi32[16:32]])
    total = total + quadratic(lower[None], rights, [phi32[32:48], phi32[48:]])
    total_ref[...] = cell_total * total


def make_maps(rows_total, cell_total, half, order, own, mine, other, basis):
    cells = basis.shape[1]
    params = order.shape[0]
    return pl.pallas_call(
        functools.partial(maps_kernel, rows_total, cell_total),
        in_specs=[SMEM, SMEM, VMEM, VMEM, VMEM, VMEM],
        out_specs=(VMEM, VMEM),
        out_shape=(jax.ShapeDtypeStruct((params, cells), F32), jax.ShapeDtypeStruct((1, cells), F32)),
        compiler_params=pltpu.CompilerParams(vmem_limit_bytes=32 << 20),
        cost_estimate=pl.CostEstimate(flops=1 << 28, bytes_accessed=1 << 20, transcendentals=0),
        name="maps",
    )(half, order, own, mine, other, basis)


def shifted(value, axis, size, shift):
    return lax.ppermute(value, axis, [(i, (i + shift) % size) for i in range(size)])


def on_device(fields, scales, pod_basis, param_order):
    rows, slots, cells = fields.shape
    blocks = scales.shape[2]
    modes = pod_basis.shape[1]
    sizes = {name: lax.axis_size(name) for name in ("grp", "z", "y", "core")}
    rows_total = float(rows * sizes["grp"])
    cell_total = float(cells * sizes["z"] * sizes["y"] * sizes["core"])
    core = lax.axis_index("core").astype(jnp.int32)
    slot = (lax.axis_index("y") * sizes["z"] + lax.axis_index("z")).astype(jnp.int32)
    by_slot = jnp.transpose(scales, (1, 2, 0)).reshape(slots * blocks, rows)
    basis = pod_basis.T

    height = lax.axis_index("y").astype(jnp.int32)
    theirs = project(jnp.stack([1 - core, height]), fields, by_slot, basis, 56)
    got = shifted(theirs, "core", 2, 1)
    where = jnp.stack([core, height])
    ours = project(where, fields, by_slot, basis)
    pieces = combine(where, ours, got)
    parts = add_up([pieces[0]] + [shifted(pieces[s], "y", sizes["y"], s) for s in range(1, sizes["y"])])
    parts = lax.all_to_all(parts, "z", 0, 0, tiled=True)

    keep, send = moments(jnp.stack([slot, core]), parts)
    piece = keep + shifted(send, "core", 2, 1)
    piece = piece + sum(shifted(piece, "grp", sizes["grp"], s) for s in range(1, sizes["grp"]))
    copies = jnp.broadcast_to(piece[None], (slots,) + piece.shape)
    mine = lax.all_to_all(copies, ("y", "z"), 0, 0, tiled=True)
    other = shifted(mine, "core", 2, 1)
    own = own_maps(core[None], mine, basis)
    sobol, total = make_maps(rows_total, cell_total, core[None], param_order, own, mine, other, basis)
    return sobol, total.reshape(cells)


def solution(mesh):
    split = Mesh(mesh.devices.reshape(4, 8, 4, 2), ("grp", "z", "y", "core"))
    cell = ("z", "y", "core")
    return jax.shard_map(
        on_device,
        mesh=split,
        in_specs=(P("grp", None, cell), P("grp", None, cell), P(cell, None), P()),
        out_specs=(P(None, cell), P(cell)),
        check_vma=False,
    )
```

```python
import functools

import jax
import jax.numpy as jnp
from jax import lax
from jax.experimental import pallas as pl
from jax.experimental.pallas import tpu as pltpu
from jax.sharding import Mesh, PartitionSpec as P

HIGHEST = lax.Precision.HIGHEST
F32 = jnp.float32
BF16 = jnp.bfloat16
VMEM = pl.BlockSpec(memory_space=pltpu.VMEM)
SMEM = pl.BlockSpec(memory_space=pltpu.SMEM)


def project_kernel(chunk, half_ref, height_ref, fields_ref, scale_ref, basis_ref, out_ref, buffer, weights, spread, scales3, sems):
    rows, slots, cells = buffer.shape
    packed = rows // 2
    modes = basis_ref.shape[0]
    lanes = 128
    blocks = cells // lanes
    chunks = packed // chunk
    groups = slots // 8
    base = half_ref[0] * rows

    def fetch(index, which):
        first = which * packed + index * chunk
        return pltpu.make_async_copy(
            fields_ref.at[pl.ds(base + first, chunk)], buffer.at[pl.ds(first, chunk)], sems.at[index, which]
        )

    for index in range(chunks):
        for which in range(2):
            fetch(index, which).start()

    weights[...] = basis_ref[...].astype(F32).T.astype(BF16)
    block_of_row = lax.broadcasted_iota(jnp.int32, (256, lanes), 0) % blocks
    for block in range(blocks):
        spread[:, block * lanes : (block + 1) * lanes] = jnp.where(block_of_row == block, 1.0, 0.0).astype(BF16)
    by_row = scale_ref[...].T
    high = by_row.astype(BF16).astype(F32)
    rest = by_row - high
    middle = rest.astype(BF16).astype(F32)
    low = rest - middle
    lane = lax.broadcasted_iota(jnp.int32, (by_row.shape[0], 128), 1)
    for q in range(groups):
        cut = slice(q // 2 * 128, q // 2 * 128 + 128)
        turned_middle = pltpu.roll(middle[:, cut], 64, 1)
        if q % 2 == 0:
            scales3[q, :, :128] = jnp.where(lane < 64, high[:, cut], turned_middle)
        else:
            scales3[q, :, :128] = jnp.where(lane < 64, turned_middle, high[:, cut])
        scales3[q, :, 128:] = low[:, cut]

    slot8 = lax.broadcasted_iota(jnp.int32, (8, 256), 0)
    lane8 = lax.broadcasted_iota(jnp.int32, (8, 256), 1)
    own = (lane8 % 64) // 8 == slot8
    masks = (own & (lane8 < 192), own & ((lane8 < 128) | (lane8 >= 192)))
    slot = lax.broadcasted_iota(jnp.int32, (slots, 2 * modes), 0)
    for index in range(chunks):
        left, pieces = [], []
        for which in range(2):
            fetch(index, which).wait()
            first = which * packed + index * chunk
            for row in range(chunk):
                for q in range(groups):
                    line = jnp.broadcast_to(scales3[q, pl.ds(base + first + row, 1), :], (8, 256))
                    left.append(jnp.where(masks[q % 2], line, 0.0))
            pieces.append(buffer[first : first + chunk].astype(F32).reshape(chunk * slots, cells))
        left = jnp.concatenate(left, axis=0).astype(BF16)
        scale = jnp.dot(left, spread[...], preferred_element_type=F32)
        dequant = (jnp.concatenate(pieces, axis=0) * scale).astype(BF16)
        product = jnp.dot(dequant, weights[...], preferred_element_type=F32)
        total = jnp.concatenate([product[: chunk * slots], product[chunk * slots :]], axis=1)
        tiles = []
        for row in range(chunk):
            tile = total[row * slots : (row + 1) * slots]
            tiles.append(tile - jnp.where(slot >= 2, jnp.broadcast_to(tile[:1], tile.shape), 0.0))
        turned = jnp.swapaxes(jnp.stack(tiles), 0, 1)
        for group in range(4):
            place = lax.rem(group + 4 - height_ref[0], 4)
            out_ref[place, :, index * chunk : (index + 1) * chunk, :] = turned[8 * group : 8 * group + 8]

def project(half, height, fields, scales, basis, room):
    rows, slots, cells = fields.shape
    modes = basis.shape[0]
    packed = rows // 4
    chunk = 16
    chunks = packed // chunk
    return pl.pallas_call(
        functools.partial(project_kernel, chunk),
        in_specs=[SMEM, SMEM, pl.BlockSpec(memory_space=pl.ANY), VMEM, VMEM],
        out_specs=VMEM,
        out_shape=jax.ShapeDtypeStruct((4, slots // 4, packed, 2 * modes), F32),
        scratch_shapes=[
            pltpu.VMEM((rows // 2, slots, cells), BF16),
            pltpu.VMEM((cells, modes), BF16),
            pltpu.VMEM((256, cells), BF16),
            pltpu.VMEM((slots // 8, rows, 256), F32),
            pltpu.SemaphoreType.DMA((chunks, 2)),
        ],
        compiler_params=pltpu.CompilerParams(vmem_limit_bytes=room << 20),
        cost_estimate=pl.CostEstimate(
            flops=rows * slots * cells * modes, bytes_accessed=rows * slots * cells, transcendentals=0
        ),
        name="project",
    )(half, height, fields, scales, basis)


def combine_kernel(height_ref, ours_ref, got_ref, *outs):
    place = lax.rem(4 - height_ref[0], 4)
    second = ours_ref[place, 1] + got_ref[place, 1]
    for group, out in enumerate(outs):
        out[:8] = ours_ref[group] + got_ref[group]
        out[8] = second


def combine(height, ours, got):
    groups, count, packed, lanes = ours.shape
    out = jax.ShapeDtypeStruct((count + 1, packed, lanes), F32)
    return pl.pallas_call(
        combine_kernel,
        in_specs=[SMEM, VMEM, VMEM],
        out_specs=[VMEM] * groups,
        out_shape=[out] * groups,
        compiler_params=pltpu.CompilerParams(vmem_limit_bytes=16 << 20),
        cost_estimate=pl.CostEstimate(flops=1 << 18, bytes_accessed=1 << 21, transcendentals=0),
        name="combine",
    )(height, ours, got)


def add_up_kernel(*refs):
    *parts, out_ref = refs
    total = parts[0][...]
    for part in parts[1:]:
        total = total + part[...]
    packed = total.shape[1]
    out_ref[:, :packed] = total[:8]
    out_ref[:, packed:] = jnp.broadcast_to(total[8:], total[:8].shape)


def add_up(parts):
    count, packed, lanes = parts[0].shape
    return pl.pallas_call(
        add_up_kernel,
        in_specs=[VMEM] * len(parts),
        out_specs=VMEM,
        out_shape=jax.ShapeDtypeStruct((count - 1, 2 * packed, lanes), F32),
        compiler_params=pltpu.CompilerParams(vmem_limit_bytes=16 << 20),
        cost_estimate=pl.CostEstimate(flops=1 << 18, bytes_accessed=1 << 20, transcendentals=0),
        name="add_up",
    )(*parts)


def moments_kernel(slot_ref, half_ref, parts_ref, keep_ref, send_ref):
    slot, half = slot_ref[0], half_ref[0]
    both = parts_ref[0]
    for source in range(1, parts_ref.shape[0]):
        both = both + parts_ref[source]
    own, second = both[:32], both[32:]
    left = jnp.where(slot == 0, own, second)
    wide = lax.dot_general(left, own, (((0,), (0,)), ((), ())), precision=HIGHEST, preferred_element_type=F32)
    matrix = wide[:64, :64] + wide[64:, 64:]
    sums = jnp.sum(own, axis=0, keepdims=True)
    sums = sums[:, :64] + sums[:, 64:]
    low = jnp.concatenate([sums[:, 32:], sums[:, :32]], axis=1)
    row = lax.broadcasted_iota(jnp.int32, matrix.shape, 0)
    lane = lax.broadcasted_iota(jnp.int32, matrix.shape, 1)
    spare = (slot < 2) & (lane < 32)
    matrix = jnp.where(spare & (row == 32), jnp.broadcast_to(sums, matrix.shape), matrix)
    matrix = jnp.where(spare & (row == 33), jnp.broadcast_to(low, matrix.shape), matrix)
    upper = jnp.concatenate([matrix[:16], matrix[16:32]], axis=1)
    lower = jnp.concatenate([matrix[32:48], matrix[48:]], axis=1)
    keep_ref[...] = jnp.where(half == 0, upper, lower)
    send_ref[...] = jnp.where(half == 0, lower, upper)


def moments(slot, half, parts):
    out = jax.ShapeDtypeStruct((16, 128), F32)
    return pl.pallas_call(
        moments_kernel,
        in_specs=[SMEM, SMEM, VMEM],
        out_specs=(VMEM, VMEM),
        out_shape=(out, out),
        compiler_params=pltpu.CompilerParams(vmem_limit_bytes=16 << 20),
        cost_estimate=pl.CostEstimate(flops=1 << 22, bytes_accessed=1 << 20, transcendentals=0),
        name="moments",
    )(slot, half, parts)


def three(value):
    high = value.astype(BF16)
    rest = value - high.astype(F32)
    middle = rest.astype(BF16)
    return high, middle, (rest - middle.astype(F32)).astype(BF16)


def right_sides(phi):
    none = jnp.zeros_like(phi)
    return (
        jnp.concatenate([phi, phi, phi, none], axis=0),
        jnp.concatenate([phi, phi, none, phi], axis=0),
    )


def quadratic(piece, rights, rows):
    count = piece.shape[0]
    cells = rights[0].shape[1]
    flat = piece.reshape(count * 16, 128)
    lane = lax.broadcasted_iota(jnp.int32, flat.shape, 1)
    high = flat.astype(BF16).astype(F32)
    rest = flat - high
    middle = rest.astype(BF16).astype(F32)
    low = (rest - middle).astype(BF16)
    turned = pltpu.roll(middle, 64, 1)
    result = None
    for side, right in enumerate(rights):
        front = jnp.where((lane < 64) == (side == 0), high, turned).astype(BF16)
        left = jnp.concatenate([front, low], axis=1)
        product = jnp.dot(left, right, preferred_element_type=F32).reshape(count, 16, cells)
        term = jnp.sum(product * rows[side], axis=1)
        result = term if result is None else result + term
    return result


def half_rows(phi32, second):
    return [
        jnp.where(second, phi32[32 + 16 * side : 48 + 16 * side], phi32[16 * side : 16 + 16 * side])
        for side in range(2)
    ]


def own_maps_kernel(half_ref, mine_ref, basis_ref, out_ref):
    rights = right_sides(basis_ref[...])
    rows = [r[None] for r in half_rows(basis_ref[...].astype(F32), half_ref[0] == 1)]
    for start in range(0, out_ref.shape[0], 8):
        out_ref[start : start + 8] = quadratic(mine_ref[start : start + 8], rights, rows)


def own_maps(half, mine, basis):
    return pl.pallas_call(
        own_maps_kernel,
        in_specs=[SMEM, VMEM, VMEM],
        out_specs=VMEM,
        out_shape=jax.ShapeDtypeStruct((mine.shape[0], basis.shape[1]), F32),
        compiler_params=pltpu.CompilerParams(vmem_limit_bytes=32 << 20),
        cost_estimate=pl.CostEstimate(flops=1 << 28, bytes_accessed=1 << 20, transcendentals=0),
        name="own_maps",
    )(half, mine, basis)


def maps_kernel(rows_total, cell_total, half_ref, order_ref, own_ref, mine_ref, other_ref, basis_ref, maps_ref, total_ref):
    half = half_ref[0]
    rights = right_sides(basis_ref[...])
    phi32 = basis_ref[...].astype(F32)
    rows = half_rows(phi32, half == 0)
    mine = mine_ref[0] + mine_ref[1]
    other = other_ref[0] + other_ref[1]
    upper, lower = jnp.where(half == 0, mine, other), jnp.where(half == 0, other, mine)
    sums = lower[0:1, :64]
    low = lower[1:2, :64]
    lane1 = lax.broadcasted_iota(jnp.int32, sums.shape, 1)
    sums = jnp.where(lane1 < 32, sums, jnp.concatenate([low[:, 32:], low[:, :32]], axis=1))
    average = jnp.broadcast_to(sums / (2.0 * rows_total), (64, 64))
    outer = average.T * average
    lane = lax.broadcasted_iota(jnp.int32, upper.shape, 1)
    column = jnp.where(lane < 64, lane, lane - 64)
    weight = jnp.where(column < 32, 1.0, 2.0)
    outer_upper = jnp.concatenate([outer[:16], outer[16:32]], axis=1)
    outer_lower = jnp.concatenate([outer[32:48], outer[48:]], axis=1)
    upper = (upper / (2.0 * rows_total) - outer_upper) * weight
    lower = jnp.where(column < 32, 0.0, lower / (2.0 * rows_total) - outer_lower)

    for start in range(0, other_ref.shape[0], 8):
        if start == 0:
            piece = jnp.concatenate([upper[None], lower[None], other_ref[2:8]], axis=0)
            first = [
                jnp.stack([phi32[16 * side : 16 * side + 16], phi32[32 + 16 * side : 48 + 16 * side]] + [rows[side]] * 6)
                for side in range(2)
            ]
            found = quadratic(piece, rights, first)
            total_ref[...] = cell_total * (found[0:1] + found[1:2])
        else:
            found = quadratic(other_ref[start : start + 8], rights, [r[None] for r in rows])
        found = cell_total / rows_total * (own_ref[start : start + 8] + found)
        for slot in range(max(start, 2), start + 8):
            maps_ref[pl.ds(order_ref[slot - 2], 1), :] = found[slot - start : slot - start + 1]


def make_maps(rows_total, cell_total, half, order, own, mine, other, basis):
    cells = basis.shape[1]
    params = order.shape[0]
    return pl.pallas_call(
        functools.partial(maps_kernel, rows_total, cell_total),
        in_specs=[SMEM, SMEM, VMEM, VMEM, VMEM, VMEM],
        out_specs=(VMEM, VMEM),
        out_shape=(jax.ShapeDtypeStruct((params, cells), F32), jax.ShapeDtypeStruct((1, cells), F32)),
        compiler_params=pltpu.CompilerParams(vmem_limit_bytes=32 << 20),
        cost_estimate=pl.CostEstimate(flops=1 << 28, bytes_accessed=1 << 20, transcendentals=0),
        name="maps",
    )(half, order, own, mine, other, basis)


def shifted(value, axis, size, shift):
    return lax.ppermute(value, axis, [(i, (i + shift) % size) for i in range(size)])


def on_device(fields, scales, pod_basis, param_order):
    rows, slots, cells = fields.shape
    blocks = scales.shape[2]
    modes = pod_basis.shape[1]
    sizes = {name: lax.axis_size(name) for name in ("grp", "z", "y", "core")}
    rows_total = float(rows * sizes["grp"])
    cell_total = float(cells * sizes["z"] * sizes["y"] * sizes["core"])
    core = lax.axis_index("core").astype(jnp.int32)
    slot = (lax.axis_index("y") * sizes["z"] + lax.axis_index("z")).astype(jnp.int32)
    by_slot = jnp.transpose(scales, (1, 2, 0)).reshape(slots * blocks, rows)
    basis = pod_basis.T

    height = lax.axis_index("y").astype(jnp.int32)[None]
    theirs = project((1 - core)[None], height, fields, by_slot, basis, 56)
    got = shifted(theirs, "core", 2, 1)
    ours = project(core[None], height, fields, by_slot, basis, 52)
    pieces = combine(height, ours, got)
    parts = add_up([pieces[0]] + [shifted(pieces[s], "y", sizes["y"], s) for s in (2, 1, 3)])
    parts = lax.all_to_all(parts, "z", 0, 0, tiled=True)

    keep, send = moments(slot[None], core[None], parts)
    piece = keep + shifted(send, "core", 2, 1)
    piece = piece + sum(shifted(piece, "grp", sizes["grp"], s) for s in range(1, sizes["grp"]))
    copies = jnp.broadcast_to(piece[None], (slots,) + piece.shape)
    mine = lax.all_to_all(copies, ("y", "z"), 0, 0, tiled=True)
    other = shifted(mine, "core", 2, 1)
    own = own_maps(core[None], mine, basis)
    sobol, total = make_maps(rows_total, cell_total, core[None], param_order, own, mine, other, basis)
    return sobol, total.reshape(cells)


def solution(mesh):
    split = Mesh(mesh.devices.reshape(4, 8, 4, 2), ("grp", "z", "y", "core"))
    cell = ("z", "y", "core")
    return jax.shard_map(
        on_device,
        mesh=split,
        in_specs=(P("grp", None, cell), P("grp", None, cell), P(cell, None), P()),
        out_specs=(P(None, cell), P(cell)),
        check_vma=False,
    )
```

```python
import functools

import jax
import jax.numpy as jnp
from jax import lax
from jax.experimental import pallas as pl
from jax.experimental.pallas import tpu as pltpu
from jax.sharding import Mesh, PartitionSpec as P

HIGHEST = lax.Precision.HIGHEST
F32 = jnp.float32
BF16 = jnp.bfloat16
VMEM = pl.BlockSpec(memory_space=pltpu.VMEM)
SMEM = pl.BlockSpec(memory_space=pltpu.SMEM)


def project_kernel(
    chunk, half_ref, height_ref, fields_ref, scale_in, basis_in, out_ref,
    buffer, scale_ref, basis_ref, weights, spread, scales3, scale_rows, dequant, sems, small_sems,
):
    rows, slots, cells = buffer.shape
    packed = rows // 2
    modes = basis_ref.shape[0]
    lanes = 128
    blocks = cells // lanes
    chunks = packed // chunk
    groups = slots // 8
    base = half_ref[0] * rows

    def fetch(index, which):
        first = which * packed + index * chunk
        return pltpu.make_async_copy(
            fields_ref.at[pl.ds(base + first, chunk)], buffer.at[pl.ds(first, chunk)], sems.at[index, which]
        )

    small = [
        pltpu.make_async_copy(scale_in, scale_ref, small_sems.at[0]),
        pltpu.make_async_copy(basis_in, basis_ref, small_sems.at[1]),
    ]
    for copy in small:
        copy.start()
    for index in range(chunks):
        for which in range(2):
            fetch(index, which).start()

    block_of_row = lax.broadcasted_iota(jnp.int32, (256, lanes), 0) % blocks
    for block in range(blocks):
        spread[:, block * lanes : (block + 1) * lanes] = jnp.where(block_of_row == block, 1.0, 0.0).astype(BF16)
    for copy in small:
        copy.wait()
    weights[...] = basis_ref[...].astype(F32).T.astype(BF16)
    by_row = scale_ref[...].T
    high = by_row.astype(BF16).astype(F32)
    rest = by_row - high
    middle = rest.astype(BF16).astype(F32)
    low = rest - middle
    lane = lax.broadcasted_iota(jnp.int32, (by_row.shape[0], 128), 1)
    for q in range(groups):
        cut = slice(q // 2 * 128, q // 2 * 128 + 128)
        turned_middle = pltpu.roll(middle[:, cut], 64, 1)
        if q % 2 == 0:
            scales3[q, :, :128] = jnp.where(lane < 64, high[:, cut], turned_middle)
        else:
            scales3[q, :, :128] = jnp.where(lane < 64, turned_middle, high[:, cut])
        scales3[q, :, 128:] = low[:, cut]

    slot8 = lax.broadcasted_iota(jnp.int32, (8, 256), 0)
    lane8 = lax.broadcasted_iota(jnp.int32, (8, 256), 1)
    own = (lane8 % 64) // 8 == slot8
    masks = (own & (lane8 < 192), own & ((lane8 < 128) | (lane8 >= 192)))
    slot = lax.broadcasted_iota(jnp.int32, (slots, 2 * modes), 0)
    few = 4
    wide = 256
    for index in range(chunks):
        for which in range(2):
            fetch(index, which).wait()
            first = which * packed + index * chunk
            for row in range(0, chunk, few):
                left = []
                for line_row in range(first + row, first + row + few):
                    for q in range(groups):
                        line = jnp.broadcast_to(scales3[q, pl.ds(base + line_row, 1), :], (8, 256))
                        left.append(jnp.where(masks[q % 2], line, 0.0))
                scale_rows[(which * chunk + row) * slots : (which * chunk + row + few) * slots] = jnp.concatenate(
                    left, axis=0
                ).astype(BF16)
        for column in range(0, cells, wide):
            for which in range(2):
                first = which * packed + index * chunk
                for row in range(0, chunk, few):
                    place = slice((which * chunk + row) * slots, (which * chunk + row + few) * slots)
                    scale = jnp.dot(
                        scale_rows[place], spread[:, column : column + wide], preferred_element_type=F32
                    )
                    piece = buffer[first + row : first + row + few, :, column : column + wide]
                    piece = piece.astype(F32).reshape(few * slots, wide)
                    dequant[place, column : column + wide] = (piece * scale).astype(BF16)
        product = jnp.dot(dequant[...], weights[...], preferred_element_type=F32)
        total = jnp.concatenate([product[: chunk * slots], product[chunk * slots :]], axis=1)
        tiles = []
        for row in range(chunk):
            tile = total[row * slots : (row + 1) * slots]
            tiles.append(tile - jnp.where(slot >= 2, jnp.broadcast_to(tile[:1], tile.shape), 0.0))
        turned = jnp.swapaxes(jnp.stack(tiles), 0, 1)
        for group in range(4):
            place = lax.rem(group + 4 - height_ref[0], 4)
            out_ref[place, :, index * chunk : (index + 1) * chunk, :] = turned[8 * group : 8 * group + 8]

def project(half, height, fields, scales, basis, room):
    rows, slots, cells = fields.shape
    modes = basis.shape[0]
    packed = rows // 4
    chunk = 16
    chunks = packed // chunk
    return pl.pallas_call(
        functools.partial(project_kernel, chunk),
        in_specs=[SMEM, SMEM] + [pl.BlockSpec(memory_space=pl.ANY)] * 3,
        out_specs=VMEM,
        out_shape=jax.ShapeDtypeStruct((4, slots // 4, packed, 2 * modes), F32),
        scratch_shapes=[
            pltpu.VMEM((rows // 2, slots, cells), BF16),
            pltpu.VMEM(scales.shape, F32),
            pltpu.VMEM(basis.shape, BF16),
            pltpu.VMEM((cells, modes), BF16),
            pltpu.VMEM((256, cells), BF16),
            pltpu.VMEM((slots // 8, rows, 256), F32),
            pltpu.VMEM((2 * chunk * slots, 256), BF16),
            pltpu.VMEM((2 * chunk * slots, cells), BF16),
            pltpu.SemaphoreType.DMA((chunks, 2)),
            pltpu.SemaphoreType.DMA((2,)),
        ],
        compiler_params=pltpu.CompilerParams(vmem_limit_bytes=room << 20),
        cost_estimate=pl.CostEstimate(
            flops=rows * slots * cells * modes, bytes_accessed=rows * slots * cells, transcendentals=0
        ),
        name="project",
    )(half, height, fields, scales, basis)


def combine_kernel(height_ref, ours_ref, got_ref, *outs):
    place = lax.rem(4 - height_ref[0], 4)
    second = ours_ref[place, 1] + got_ref[place, 1]
    for group, out in enumerate(outs):
        out[:8] = ours_ref[group] + got_ref[group]
        out[8] = second


def combine(height, ours, got):
    groups, count, packed, lanes = ours.shape
    out = jax.ShapeDtypeStruct((count + 1, packed, lanes), F32)
    return pl.pallas_call(
        combine_kernel,
        in_specs=[SMEM, VMEM, VMEM],
        out_specs=[VMEM] * groups,
        out_shape=[out] * groups,
        compiler_params=pltpu.CompilerParams(vmem_limit_bytes=16 << 20),
        cost_estimate=pl.CostEstimate(flops=1 << 18, bytes_accessed=1 << 21, transcendentals=0),
        name="combine",
    )(height, ours, got)


def add_up_kernel(*refs):
    *parts, out_ref = refs
    total = parts[0][...]
    for part in parts[1:]:
        total = total + part[...]
    packed = total.shape[1]
    out_ref[:, :packed] = total[:8]
    out_ref[:, packed:] = jnp.broadcast_to(total[8:], total[:8].shape)


def add_up(parts):
    count, packed, lanes = parts[0].shape
    return pl.pallas_call(
        add_up_kernel,
        in_specs=[VMEM] * len(parts),
        out_specs=VMEM,
        out_shape=jax.ShapeDtypeStruct((count - 1, 2 * packed, lanes), F32),
        compiler_params=pltpu.CompilerParams(vmem_limit_bytes=16 << 20),
        cost_estimate=pl.CostEstimate(flops=1 << 18, bytes_accessed=1 << 20, transcendentals=0),
        name="add_up",
    )(*parts)


def moments_kernel(slot_ref, half_ref, parts_ref, keep_ref, send_ref):
    slot, half = slot_ref[0], half_ref[0]
    both = parts_ref[0]
    for source in range(1, parts_ref.shape[0]):
        both = both + parts_ref[source]
    own, second = both[:32], both[32:]
    left = jnp.where(slot == 0, own, second)
    wide = lax.dot_general(left, own, (((0,), (0,)), ((), ())), precision=HIGHEST, preferred_element_type=F32)
    matrix = wide[:64, :64] + wide[64:, 64:]
    sums = jnp.sum(own, axis=0, keepdims=True)
    sums = sums[:, :64] + sums[:, 64:]
    low = jnp.concatenate([sums[:, 32:], sums[:, :32]], axis=1)
    row = lax.broadcasted_iota(jnp.int32, matrix.shape, 0)
    lane = lax.broadcasted_iota(jnp.int32, matrix.shape, 1)
    spare = (slot < 2) & (lane < 32)
    matrix = jnp.where(spare & (row == 32), jnp.broadcast_to(sums, matrix.shape), matrix)
    matrix = jnp.where(spare & (row == 33), jnp.broadcast_to(low, matrix.shape), matrix)
    upper = jnp.concatenate([matrix[:16], matrix[16:32]], axis=1)
    lower = jnp.concatenate([matrix[32:48], matrix[48:]], axis=1)
    keep_ref[...] = jnp.where(half == 0, upper, lower)
    send_ref[...] = jnp.where(half == 0, lower, upper)


def moments(slot, half, parts):
    out = jax.ShapeDtypeStruct((16, 128), F32)
    return pl.pallas_call(
        moments_kernel,
        in_specs=[SMEM, SMEM, VMEM],
        out_specs=(VMEM, VMEM),
        out_shape=(out, out),
        compiler_params=pltpu.CompilerParams(vmem_limit_bytes=16 << 20),
        cost_estimate=pl.CostEstimate(flops=1 << 22, bytes_accessed=1 << 20, transcendentals=0),
        name="moments",
    )(slot, half, parts)


def three(value):
    high = value.astype(BF16)
    rest = value - high.astype(F32)
    middle = rest.astype(BF16)
    return high, middle, (rest - middle.astype(F32)).astype(BF16)


def right_sides(phi):
    none = jnp.zeros_like(phi)
    return (
        jnp.concatenate([phi, phi, phi, none], axis=0),
        jnp.concatenate([phi, phi, none, phi], axis=0),
    )


def quadratic(piece, rights, rows):
    count = piece.shape[0]
    cells = rights[0].shape[1]
    flat = piece.reshape(count * 16, 128)
    lane = lax.broadcasted_iota(jnp.int32, flat.shape, 1)
    high = flat.astype(BF16).astype(F32)
    rest = flat - high
    middle = rest.astype(BF16).astype(F32)
    low = (rest - middle).astype(BF16)
    turned = pltpu.roll(middle, 64, 1)
    result = None
    for side, right in enumerate(rights):
        front = jnp.where((lane < 64) == (side == 0), high, turned).astype(BF16)
        left = jnp.concatenate([front, low], axis=1)
        product = jnp.dot(left, right, preferred_element_type=F32).reshape(count, 16, cells)
        term = jnp.sum(product * rows[side], axis=1)
        result = term if result is None else result + term
    return result


def half_rows(phi32, second):
    return [
        jnp.where(second, phi32[32 + 16 * side : 48 + 16 * side], phi32[16 * side : 16 + 16 * side])
        for side in range(2)
    ]


def own_maps_kernel(half_ref, mine_ref, basis_ref, out_ref):
    rights = right_sides(basis_ref[...])
    rows = [r[None] for r in half_rows(basis_ref[...].astype(F32), half_ref[0] == 1)]
    for start in range(0, out_ref.shape[0], 8):
        out_ref[start : start + 8] = quadratic(mine_ref[start : start + 8], rights, rows)


def own_maps(half, mine, basis):
    return pl.pallas_call(
        own_maps_kernel,
        in_specs=[SMEM, VMEM, VMEM],
        out_specs=VMEM,
        out_shape=jax.ShapeDtypeStruct((mine.shape[0], basis.shape[1]), F32),
        compiler_params=pltpu.CompilerParams(vmem_limit_bytes=32 << 20),
        cost_estimate=pl.CostEstimate(flops=1 << 28, bytes_accessed=1 << 20, transcendentals=0),
        name="own_maps",
    )(half, mine, basis)


def maps_kernel(rows_total, cell_total, half_ref, order_ref, own_ref, mine_ref, other_ref, basis_ref, maps_ref, total_ref):
    half = half_ref[0]
    rights = right_sides(basis_ref[...])
    phi32 = basis_ref[...].astype(F32)
    rows = half_rows(phi32, half == 0)
    mine = mine_ref[0] + mine_ref[1]
    other = other_ref[0] + other_ref[1]
    upper, lower = jnp.where(half == 0, mine, other), jnp.where(half == 0, other, mine)
    sums = lower[0:1, :64]
    low = lower[1:2, :64]
    lane1 = lax.broadcasted_iota(jnp.int32, sums.shape, 1)
    sums = jnp.where(lane1 < 32, sums, jnp.concatenate([low[:, 32:], low[:, :32]], axis=1))
    average = jnp.broadcast_to(sums / (2.0 * rows_total), (64, 64))
    outer = average.T * average
    lane = lax.broadcasted_iota(jnp.int32, upper.shape, 1)
    column = jnp.where(lane < 64, lane, lane - 64)
    weight = jnp.where(column < 32, 1.0, 2.0)
    outer_upper = jnp.concatenate([outer[:16], outer[16:32]], axis=1)
    outer_lower = jnp.concatenate([outer[32:48], outer[48:]], axis=1)
    upper = (upper / (2.0 * rows_total) - outer_upper) * weight
    lower = jnp.where(column < 32, 0.0, lower / (2.0 * rows_total) - outer_lower)

    for start in range(0, other_ref.shape[0], 8):
        if start == 0:
            piece = jnp.concatenate([upper[None], lower[None], other_ref[2:8]], axis=0)
            first = [
                jnp.stack([phi32[16 * side : 16 * side + 16], phi32[32 + 16 * side : 48 + 16 * side]] + [rows[side]] * 6)
                for side in range(2)
            ]
            found = quadratic(piece, rights, first)
            total_ref[...] = cell_total * (found[0:1] + found[1:2])
        else:
            found = quadratic(other_ref[start : start + 8], rights, [r[None] for r in rows])
        found = cell_total / rows_total * (own_ref[start : start + 8] + found)
        for slot in range(max(start, 2), start + 8):
            maps_ref[pl.ds(order_ref[slot - 2], 1), :] = found[slot - start : slot - start + 1]


def make_maps(rows_total, cell_total, half, order, own, mine, other, basis):
    cells = basis.shape[1]
    params = order.shape[0]
    return pl.pallas_call(
        functools.partial(maps_kernel, rows_total, cell_total),
        in_specs=[SMEM, SMEM, VMEM, VMEM, VMEM, VMEM],
        out_specs=(VMEM, VMEM),
        out_shape=(jax.ShapeDtypeStruct((params, cells), F32), jax.ShapeDtypeStruct((1, cells), F32)),
        compiler_params=pltpu.CompilerParams(vmem_limit_bytes=32 << 20),
        cost_estimate=pl.CostEstimate(flops=1 << 28, bytes_accessed=1 << 20, transcendentals=0),
        name="maps",
    )(half, order, own, mine, other, basis)


def shifted(value, axis, size, shift):
    return lax.ppermute(value, axis, [(i, (i + shift) % size) for i in range(size)])


def on_device(fields, scales, pod_basis, param_order):
    rows, slots, cells = fields.shape
    blocks = scales.shape[2]
    modes = pod_basis.shape[1]
    sizes = {name: lax.axis_size(name) for name in ("grp", "z", "y", "core")}
    rows_total = float(rows * sizes["grp"])
    cell_total = float(cells * sizes["z"] * sizes["y"] * sizes["core"])
    core = lax.axis_index("core").astype(jnp.int32)
    slot = (lax.axis_index("y") * sizes["z"] + lax.axis_index("z")).astype(jnp.int32)
    by_slot = jnp.transpose(scales, (1, 2, 0)).reshape(slots * blocks, rows)
    basis = pod_basis.T

    height = lax.axis_index("y").astype(jnp.int32)[None]
    theirs = project((1 - core)[None], height, fields, by_slot, basis, 56)
    got = shifted(theirs, "core", 2, 1)
    ours = project(core[None], height, fields, by_slot, basis, 52)
    pieces = combine(height, ours, got)
    parts = add_up([pieces[0]] + [shifted(pieces[s], "y", sizes["y"], s) for s in (2, 1, 3)])
    parts = lax.all_to_all(parts, "z", 0, 0, tiled=True)

    keep, send = moments(slot[None], core[None], parts)
    piece = keep + shifted(send, "core", 2, 1)
    piece = piece + sum(shifted(piece, "grp", sizes["grp"], s) for s in range(1, sizes["grp"]))
    copies = jnp.broadcast_to(piece[None], (slots,) + piece.shape)
    mine = lax.all_to_all(copies, ("y", "z"), 0, 0, tiled=True)
    other = shifted(mine, "core", 2, 1)
    own = own_maps(core[None], mine, basis)
    sobol, total = make_maps(rows_total, cell_total, core[None], param_order, own, mine, other, basis)
    return sobol, total.reshape(cells)


def solution(mesh):
    split = Mesh(mesh.devices.reshape(4, 8, 4, 2), ("grp", "z", "y", "core"))
    cell = ("z", "y", "core")
    return jax.shard_map(
        on_device,
        mesh=split,
        in_specs=(P("grp", None, cell), P("grp", None, cell), P(cell, None), P()),
        out_specs=(P(None, cell), P(cell)),
        check_vma=False,
    )
```

```python
import functools

import jax
import jax.numpy as jnp
from jax import lax
from jax.experimental import pallas as pl
from jax.experimental.pallas import tpu as pltpu
from jax.sharding import Mesh, PartitionSpec as P

HIGHEST = lax.Precision.HIGHEST
F32 = jnp.float32
BF16 = jnp.bfloat16
VMEM = pl.BlockSpec(memory_space=pltpu.VMEM)
SMEM = pl.BlockSpec(memory_space=pltpu.SMEM)


def project_kernel(
    chunk, half_ref, height_ref, fields_ref, scale_in, basis_in, out_ref,
    buffer, scale_ref, basis_ref, weights, spread, scales3, scale_rows, dequant, sems, small_sems,
):
    rows, slots, cells = buffer.shape
    packed = rows // 2
    modes = basis_ref.shape[0]
    lanes = 128
    blocks = cells // lanes
    chunks = packed // chunk
    groups = slots // 8
    base = half_ref[0] * rows

    def fetch(index, which):
        first = which * packed + index * chunk
        return pltpu.make_async_copy(
            fields_ref.at[pl.ds(base + first, chunk)], buffer.at[pl.ds(first, chunk)], sems.at[index, which]
        )

    small = [
        pltpu.make_async_copy(scale_in, scale_ref, small_sems.at[0]),
        pltpu.make_async_copy(basis_in, basis_ref, small_sems.at[1]),
    ]
    for copy in small:
        copy.start()
    for index in range(chunks):
        for which in range(2):
            fetch(index, which).start()

    block_of_row = lax.broadcasted_iota(jnp.int32, (256, lanes), 0) % blocks
    for block in range(blocks):
        spread[:, block * lanes : (block + 1) * lanes] = jnp.where(block_of_row == block, 1.0, 0.0).astype(BF16)
    for copy in small:
        copy.wait()
    weights[...] = basis_ref[...].astype(F32).T.astype(BF16)
    by_row = scale_ref[...].T
    high = by_row.astype(BF16).astype(F32)
    rest = by_row - high
    middle = rest.astype(BF16).astype(F32)
    low = rest - middle
    lane = lax.broadcasted_iota(jnp.int32, (by_row.shape[0], 128), 1)
    for q in range(groups):
        cut = slice(q // 2 * 128, q // 2 * 128 + 128)
        turned_middle = pltpu.roll(middle[:, cut], 64, 1)
        if q % 2 == 0:
            scales3[q, :, :128] = jnp.where(lane < 64, high[:, cut], turned_middle)
        else:
            scales3[q, :, :128] = jnp.where(lane < 64, turned_middle, high[:, cut])
        scales3[q, :, 128:] = low[:, cut]

    slot8 = lax.broadcasted_iota(jnp.int32, (8, 256), 0)
    lane8 = lax.broadcasted_iota(jnp.int32, (8, 256), 1)
    own = (lane8 % 64) // 8 == slot8
    masks = (own & (lane8 < 192), own & ((lane8 < 128) | (lane8 >= 192)))
    slot = lax.broadcasted_iota(jnp.int32, (slots, 2 * modes), 0)
    few = 4
    wide = 256
    for index in range(chunks):
        for which in range(2):
            fetch(index, which).wait()
            first = which * packed + index * chunk
            for row in range(0, chunk, few):
                left = []
                for line_row in range(first + row, first + row + few):
                    for q in range(groups):
                        line = jnp.broadcast_to(scales3[q, pl.ds(base + line_row, 1), :], (8, 256))
                        left.append(jnp.where(masks[q % 2], line, 0.0))
                scale_rows[(which * chunk + row) * slots : (which * chunk + row + few) * slots] = jnp.concatenate(
                    left, axis=0
                ).astype(BF16)
        for column in range(0, cells, wide):
            for which in range(2):
                first = which * packed + index * chunk
                for row in range(0, chunk, few):
                    place = slice((which * chunk + row) * slots, (which * chunk + row + few) * slots)
                    scale = jnp.dot(
                        scale_rows[place], spread[:, column : column + wide], preferred_element_type=F32
                    )
                    piece = buffer[first + row : first + row + few, :, column : column + wide]
                    piece = piece.astype(F32).reshape(few * slots, wide)
                    dequant[place, column : column + wide] = (piece * scale).astype(BF16)
        product = jnp.dot(dequant[...], weights[...], preferred_element_type=F32)
        total = jnp.concatenate([product[: chunk * slots], product[chunk * slots :]], axis=1)
        tiles = []
        for row in range(chunk):
            tile = total[row * slots : (row + 1) * slots]
            tiles.append(tile - jnp.where(slot >= 2, jnp.broadcast_to(tile[:1], tile.shape), 0.0))
        turned = jnp.swapaxes(jnp.stack(tiles), 0, 1)
        for group in range(4):
            place = lax.rem(group + 4 - height_ref[0], 4)
            out_ref[place, :, index * chunk : (index + 1) * chunk, :] = turned[8 * group : 8 * group + 8]

def project(half, height, fields, scales, basis, room):
    rows, slots, cells = fields.shape
    modes = basis.shape[0]
    packed = rows // 4
    chunk = 16
    chunks = packed // chunk
    return pl.pallas_call(
        functools.partial(project_kernel, chunk),
        in_specs=[SMEM, SMEM] + [pl.BlockSpec(memory_space=pl.ANY)] * 3,
        out_specs=VMEM,
        out_shape=jax.ShapeDtypeStruct((4, slots // 4, packed, 2 * modes), F32),
        scratch_shapes=[
            pltpu.VMEM((rows // 2, slots, cells), BF16),
            pltpu.VMEM(scales.shape, F32),
            pltpu.VMEM(basis.shape, BF16),
            pltpu.VMEM((cells, modes), BF16),
            pltpu.VMEM((256, cells), BF16),
            pltpu.VMEM((slots // 8, rows, 256), F32),
            pltpu.VMEM((2 * chunk * slots, 256), BF16),
            pltpu.VMEM((2 * chunk * slots, cells), BF16),
            pltpu.SemaphoreType.DMA((chunks, 2)),
            pltpu.SemaphoreType.DMA((2,)),
        ],
        compiler_params=pltpu.CompilerParams(vmem_limit_bytes=room << 20),
        cost_estimate=pl.CostEstimate(
            flops=rows * slots * cells * modes, bytes_accessed=rows * slots * cells, transcendentals=0
        ),
        name="project",
    )(half, height, fields, scales, basis)


def combine_kernel(height_ref, ours_ref, got_ref, *outs):
    place = lax.rem(4 - height_ref[0], 4)
    second = ours_ref[place, 1] + got_ref[place, 1]
    for group, out in enumerate(outs):
        out[:8] = ours_ref[group] + got_ref[group]
        out[8] = second


def combine(height, ours, got):
    groups, count, packed, lanes = ours.shape
    out = jax.ShapeDtypeStruct((count + 1, packed, lanes), F32)
    return pl.pallas_call(
        combine_kernel,
        in_specs=[SMEM, VMEM, VMEM],
        out_specs=[VMEM] * groups,
        out_shape=[out] * groups,
        compiler_params=pltpu.CompilerParams(vmem_limit_bytes=16 << 20),
        cost_estimate=pl.CostEstimate(flops=1 << 18, bytes_accessed=1 << 21, transcendentals=0),
        name="combine",
    )(height, ours, got)


def add_up_kernel(*refs):
    *parts, out_ref = refs
    total = parts[0][...]
    for part in parts[1:]:
        total = total + part[...]
    packed = total.shape[1]
    out_ref[:, :packed] = total[:8]
    out_ref[:, packed:] = jnp.broadcast_to(total[8:], total[:8].shape)


def add_up(parts):
    count, packed, lanes = parts[0].shape
    return pl.pallas_call(
        add_up_kernel,
        in_specs=[VMEM] * len(parts),
        out_specs=VMEM,
        out_shape=jax.ShapeDtypeStruct((count - 1, 2 * packed, lanes), F32),
        compiler_params=pltpu.CompilerParams(vmem_limit_bytes=16 << 20),
        cost_estimate=pl.CostEstimate(flops=1 << 18, bytes_accessed=1 << 20, transcendentals=0),
        name="add_up",
    )(*parts)


def moments_kernel(slot_ref, half_ref, parts_ref, keep_ref, send_ref):
    slot, half = slot_ref[0], half_ref[0]
    both = parts_ref[0]
    for source in range(1, parts_ref.shape[0]):
        both = both + parts_ref[source]
    own, second = both[:32], both[32:]
    left = jnp.where(slot == 0, own, second)
    wide = lax.dot_general(left, own, (((0,), (0,)), ((), ())), precision=HIGHEST, preferred_element_type=F32)
    matrix = wide[:64, :64] + wide[64:, 64:]
    sums = jnp.sum(own, axis=0, keepdims=True)
    sums = sums[:, :64] + sums[:, 64:]
    low = jnp.concatenate([sums[:, 32:], sums[:, :32]], axis=1)
    row = lax.broadcasted_iota(jnp.int32, matrix.shape, 0)
    lane = lax.broadcasted_iota(jnp.int32, matrix.shape, 1)
    spare = (slot < 2) & (lane < 32)
    matrix = jnp.where(spare & (row == 32), jnp.broadcast_to(sums, matrix.shape), matrix)
    matrix = jnp.where(spare & (row == 33), jnp.broadcast_to(low, matrix.shape), matrix)
    upper = jnp.concatenate([matrix[:16], matrix[16:32]], axis=1)
    lower = jnp.concatenate([matrix[32:48], matrix[48:]], axis=1)
    keep_ref[...] = jnp.where(half == 0, upper, lower)
    send_ref[...] = jnp.where(half == 0, lower, upper)


def moments(slot, half, parts):
    out = jax.ShapeDtypeStruct((16, 128), F32)
    return pl.pallas_call(
        moments_kernel,
        in_specs=[SMEM, SMEM, VMEM],
        out_specs=(VMEM, VMEM),
        out_shape=(out, out),
        compiler_params=pltpu.CompilerParams(vmem_limit_bytes=16 << 20),
        cost_estimate=pl.CostEstimate(flops=1 << 22, bytes_accessed=1 << 20, transcendentals=0),
        name="moments",
    )(slot, half, parts)


def three(value):
    high = value.astype(BF16)
    rest = value - high.astype(F32)
    middle = rest.astype(BF16)
    return high, middle, (rest - middle.astype(F32)).astype(BF16)


def right_sides(phi):
    none = jnp.zeros_like(phi)
    return (
        jnp.concatenate([phi, phi, phi, none], axis=0),
        jnp.concatenate([phi, phi, none, phi], axis=0),
    )


def quadratic(piece, rights, rows):
    count = piece.shape[0]
    cells = rights[0].shape[1]
    flat = piece.reshape(count * 16, 128)
    lane = lax.broadcasted_iota(jnp.int32, flat.shape, 1)
    high = flat.astype(BF16).astype(F32)
    rest = flat - high
    middle = rest.astype(BF16).astype(F32)
    low = (rest - middle).astype(BF16)
    turned = pltpu.roll(middle, 64, 1)
    result = None
    for side, right in enumerate(rights):
        front = jnp.where((lane < 64) == (side == 0), high, turned).astype(BF16)
        left = jnp.concatenate([front, low], axis=1)
        product = jnp.dot(left, right, preferred_element_type=F32).reshape(count, 16, cells)
        term = jnp.sum(product * rows[side], axis=1)
        result = term if result is None else result + term
    return result


def half_rows(phi32, second):
    return [
        jnp.where(second, phi32[32 + 16 * side : 48 + 16 * side], phi32[16 * side : 16 + 16 * side])
        for side in range(2)
    ]


def own_maps_kernel(half_ref, mine_ref, basis_ref, out_ref):
    rights = right_sides(basis_ref[...])
    rows = [r[None] for r in half_rows(basis_ref[...].astype(F32), half_ref[0] == 1)]
    for start in range(0, out_ref.shape[0], 8):
        out_ref[start : start + 8] = quadratic(mine_ref[start : start + 8], rights, rows)


def own_maps(half, mine, basis):
    return pl.pallas_call(
        own_maps_kernel,
        in_specs=[SMEM, VMEM, VMEM],
        out_specs=VMEM,
        out_shape=jax.ShapeDtypeStruct((mine.shape[0], basis.shape[1]), F32),
        compiler_params=pltpu.CompilerParams(vmem_limit_bytes=32 << 20),
        cost_estimate=pl.CostEstimate(flops=1 << 28, bytes_accessed=1 << 20, transcendentals=0),
        name="own_maps",
    )(half, mine, basis)


def maps_kernel(rows_total, cell_total, half_ref, order_ref, own_ref, mine_ref, other_ref, basis_ref, maps_ref, total_ref):
    half = half_ref[0]
    rights = right_sides(basis_ref[...])
    phi32 = basis_ref[...].astype(F32)
    rows = half_rows(phi32, half == 0)
    mine = mine_ref[0] + mine_ref[1]
    other = other_ref[0] + other_ref[1]
    upper, lower = jnp.where(half == 0, mine, other), jnp.where(half == 0, other, mine)
    sums = lower[0:1, :64]
    low = lower[1:2, :64]
    lane1 = lax.broadcasted_iota(jnp.int32, sums.shape, 1)
    sums = jnp.where(lane1 < 32, sums, jnp.concatenate([low[:, 32:], low[:, :32]], axis=1))
    average = jnp.broadcast_to(sums / (2.0 * rows_total), (64, 64))
    outer = average.T * average
    lane = lax.broadcasted_iota(jnp.int32, upper.shape, 1)
    column = jnp.where(lane < 64, lane, lane - 64)
    weight = jnp.where(column < 32, 1.0, 2.0)
    outer_upper = jnp.concatenate([outer[:16], outer[16:32]], axis=1)
    outer_lower = jnp.concatenate([outer[32:48], outer[48:]], axis=1)
    upper = (upper / (2.0 * rows_total) - outer_upper) * weight
    lower = jnp.where(column < 32, 0.0, lower / (2.0 * rows_total) - outer_lower)

    for start in range(0, other_ref.shape[0], 8):
        if start == 0:
            piece = jnp.concatenate([upper[None], lower[None], other_ref[2:8]], axis=0)
            first = [
                jnp.stack([phi32[16 * side : 16 * side + 16], phi32[32 + 16 * side : 48 + 16 * side]] + [rows[side]] * 6)
                for side in range(2)
            ]
            found = quadratic(piece, rights, first)
            total_ref[...] = cell_total * (found[0:1] + found[1:2])
        else:
            found = quadratic(other_ref[start : start + 8], rights, [r[None] for r in rows])
        found = cell_total / rows_total * (own_ref[start : start + 8] + found)
        for slot in range(max(start, 2), start + 8):
            maps_ref[pl.ds(order_ref[slot - 2], 1), :] = found[slot - start : slot - start + 1]


def make_maps(rows_total, cell_total, half, order, own, mine, other, basis):
    cells = basis.shape[1]
    params = order.shape[0]
    return pl.pallas_call(
        functools.partial(maps_kernel, rows_total, cell_total),
        in_specs=[SMEM, SMEM, VMEM, VMEM, VMEM, VMEM],
        out_specs=(VMEM, VMEM),
        out_shape=(jax.ShapeDtypeStruct((params, cells), F32), jax.ShapeDtypeStruct((1, cells), F32)),
        compiler_params=pltpu.CompilerParams(vmem_limit_bytes=32 << 20),
        cost_estimate=pl.CostEstimate(flops=1 << 28, bytes_accessed=1 << 20, transcendentals=0),
        name="maps",
    )(half, order, own, mine, other, basis)


def shifted(value, axis, size, shift):
    return lax.ppermute(value, axis, [(i, (i + shift) % size) for i in range(size)])


def on_device(fields, scales, pod_basis, param_order):
    rows, slots, cells = fields.shape
    blocks = scales.shape[2]
    modes = pod_basis.shape[1]
    sizes = {name: lax.axis_size(name) for name in ("grp", "z", "y", "core")}
    rows_total = float(rows * sizes["grp"])
    cell_total = float(cells * sizes["z"] * sizes["y"] * sizes["core"])
    core = lax.axis_index("core").astype(jnp.int32)
    slot = (lax.axis_index("y") * sizes["z"] + lax.axis_index("z")).astype(jnp.int32)
    by_slot = jnp.transpose(scales, (1, 2, 0)).reshape(slots * blocks, rows)
    basis = pod_basis.T

    height = lax.axis_index("y").astype(jnp.int32)[None]
    theirs = project((1 - core)[None], height, fields, by_slot, basis, 56)
    got = shifted(theirs, "core", 2, 1)
    ours = project(core[None], height, fields, by_slot, basis, 52)
    pieces = combine(height, ours, got)
    parts = add_up([pieces[0]] + [shifted(pieces[s], "y", sizes["y"], s) for s in (2, 1, 3)])
    parts = lax.all_to_all(parts, "z", 0, 0, tiled=True)

    keep, send = moments(slot[None], core[None], parts)
    piece = keep + shifted(send, "core", 2, 1)
    piece = piece + sum(shifted(piece, "grp", sizes["grp"], s) for s in (1, 3, 2))
    copies = jnp.broadcast_to(piece[None], (slots,) + piece.shape)
    mine = lax.all_to_all(copies, ("y", "z"), 0, 0, tiled=True)
    other = shifted(mine, "core", 2, 1)
    own = own_maps(core[None], mine, basis)
    sobol, total = make_maps(rows_total, cell_total, core[None], param_order, own, mine, other, basis)
    return sobol, total.reshape(cells)


def solution(mesh):
    split = Mesh(mesh.devices.reshape(4, 8, 4, 2), ("grp", "z", "y", "core"))
    cell = ("z", "y", "core")
    return jax.shard_map(
        on_device,
        mesh=split,
        in_specs=(P("grp", None, cell), P("grp", None, cell), P(cell, None), P()),
        out_specs=(P(None, cell), P(cell)),
        check_vma=False,
    )
```
